32 devices in a mesh: dp: 8 (over z, core), ctx: 4 (over y, x).
Axes of the slice: x: 2, y: 2, z: 4, core: 2. Of those that a mesh axis runs over, the one named last changes fastest.
Arguments:
- loader_rows: bfloat16 [8192, 512], P(('dp', 'ctx')), may hold values from -60 to 60
- send_slot: int32 [8192], P(('dp', 'ctx')), may hold values from 0 to 383, as said below
- arrive_slot: int32 [8192], P(('dp', 'ctx')), may hold values from 0 to 383, as said below
- user_lengths: int32 [8, 4], P('dp'), may hold values from 1 to 768, 1024 in all within a row
- proj_weight: bfloat16 [512, 2048], replicated, may hold values from -0.25 to 0.25
- out_weight: bfloat16 [512, 512], replicated, may hold values from -0.25 to 0.25
- cotangent: bfloat16 [8192, 512], P(('dp', 'ctx')), may hold values from -6 to 6
Outputs:
- layer_out: bfloat16 [8192, 512], P(('dp', 'ctx'))
- row_grads: bfloat16 [8192, 512], P(('dp', 'ctx'))
- proj_grad: float32 [512, 2048], replicated
- out_grad: float32 [512, 512], replicated
The draws below stay inside these ranges and needn't reach their ends.
Inputs may be any that keep to these rules, and one draw needn't show every extreme that they name: `send_slot`: on each loader device its 256 entries are distinct slots d * 12 + k, d the owner device and k counting that owner's rows from this loader from 0; no loader sends more than 12 rows to one owner and some pairs send exactly 12; the number of rows from loader s to owner d depends only on (d - s) mod (8 * 4). `arrive_slot`: on each owner device its 256 entries are distinct slots s * 12 + k, the k-th row that loader s sends to it; every owner receives exactly 256 rows.
All inputs are finite; a program needn't handle non-finite values.
Results may differ from the reference program's by a relative error of at most 0.009.
Values may be sent and summed in bfloat16 or wider, within the bound.
No kernel may reach another device: no remote copies, remote signals or barrier semaphores. Data moves between devices by JAX's collectives and lax.ppermute only.
A program may use at most 128 MiB of HBM per device.

```python
import math
import jax
import jax.numpy as jnp
import numpy as np
from jax import lax

D = 512
HEADS = 8
TOK_DEV = 256
USERS = 4
GROUP_ROWS = 1024
LONGEST = 768
GROUPS = 8
ALL_ROWS = 8192
CAP = 12
N_DP = 8
N_CTX = 4


def packing_tables(key):
    device_count = N_DP * N_CTX
    per_pair = TOK_DEV // device_count
    spread = max(1, per_pair // 2)
    capacity = per_pair + spread
    base = jax.random.fold_in(key, 71)
    shuffled = jax.random.permutation(jax.random.fold_in(base, 1), device_count).astype(jnp.int32) + 3
    distance = jnp.arange(device_count, dtype=jnp.int32)
    priority = jnp.where(distance == 1, 0, jnp.where(distance == device_count // 2, 1, jnp.where(distance == device_count - 1, 2, shuffled)))
    order = jnp.argsort(jnp.argsort(priority, stable=True), stable=True)
    offset_of = jnp.where(order < device_count // 2, spread, -spread).astype(jnp.int32)
    source_ids = jnp.arange(device_count, dtype=jnp.int32)[:, None]
    target_ids = jnp.arange(device_count, dtype=jnp.int32)[None, :]
    counts = per_pair + offset_of[(target_ids - source_ids) % device_count]
    send_start = jnp.cumsum(counts, axis=1) - counts
    send_keys = jax.random.split(jax.random.fold_in(base, 2), device_count)
    send_order = jax.vmap(lambda each: jax.random.permutation(each, TOK_DEV))(send_keys).astype(jnp.int32)
    send_ends = send_start + counts
    target = jnp.sum((send_ends[:, None, :] <= send_order[:, :, None]).astype(jnp.int32), axis=2)
    send_within = send_order - jnp.take_along_axis(send_start, target, axis=1)
    send_slot = (target * capacity + send_within).reshape(-1).astype(jnp.int32)
    arrive_start = (jnp.cumsum(counts, axis=0) - counts).T
    arrive_keys = jax.random.split(jax.random.fold_in(base, 3), device_count)
    arrive_order = jax.vmap(lambda each: jax.random.permutation(each, TOK_DEV))(arrive_keys).astype(jnp.int32)
    arrive_ends = arrive_start + counts.T
    source = jnp.sum((arrive_ends[:, None, :] <= arrive_order[:, :, None]).astype(jnp.int32), axis=2)
    arrive_within = arrive_order - jnp.take_along_axis(arrive_start, source, axis=1)
    arrive_slot = (source * capacity + arrive_within).reshape(-1).astype(jnp.int32)
    return (send_slot, arrive_slot)


def draw_send_slot(key, part):
    return packing_tables(key)[0]


def draw_arrive_slot(key, part):
    return packing_tables(key)[1]


def draw_loader_rows(key, part):
    row_total = N_DP * N_CTX * TOK_DEV
    first, second, third = jax.random.split(jax.random.fold_in(key, 5), 3)
    values = jnp.clip(jax.random.normal(first, (row_total, D), jnp.float32), -4.0, 4.0)
    row_scale = 0.5 * jnp.exp(jax.random.uniform(second, (row_total, 1), jnp.float32, 0.0, math.log(10.0)))
    col_scale = 0.3 * jnp.exp(jax.random.uniform(third, (1, D), jnp.float32, 0.0, math.log(10.0)))
    result = values * row_scale * col_scale
    return result.astype(jnp.bfloat16)


def draw_cotangent(key, part):
    row_total = N_DP * N_CTX * TOK_DEV
    first = jax.random.fold_in(jax.random.fold_in(key, 9), 0)
    result = jnp.clip(jax.random.normal(first, (row_total, D), jnp.float32), -4.0, 4.0)
    return result.astype(jnp.bfloat16)


def profile(amount, total, limit, lean):
    portions = [(1 << 20) // math.isqrt(grade ** lean) + 1 for grade in range(2, amount + 1)]
    rest, given = total - limit - (amount - 1), [1] * (amount - 1)
    while rest > 0:
        candidates = [i for i in range(amount - 1) if given[i] < limit]
        mass, left = sum([portions[i] for i in candidates]), rest
        for i in candidates:
            more = min(limit - given[i], max(1, left * portions[i] // mass), rest)
            given[i] = given[i] + more
            rest = rest - more
    return np.array([limit] + given)


def ragged_sizes(own_key, number_of, total, bound, lean):
    if number_of == 2:
        one = jax.random.randint(own_key, (), max(1, total - bound), min(bound, total - 1) + 1)
        return jnp.stack([one, total - one])
    sizes = jnp.asarray(profile(number_of, total, bound, lean), jnp.int32)
    pairs = (number_of - 1) // 2
    giver, sink = sizes[1:1 + 2 * pairs:2], sizes[2:2 + 2 * pairs:2]
    margin = jnp.minimum(giver - 1, bound - sink)
    passed = jax.random.randint(jax.random.fold_in(own_key, 1), (pairs,), 0, 1 << 20) % (margin + 1)
    sizes = sizes.at[1:1 + 2 * pairs:2].set(giver - passed).at[2:2 + 2 * pairs:2].set(sink + passed)
    return sizes[jax.random.permutation(jax.random.fold_in(own_key, 2), number_of)]


def normal_values(rng, shape, scale, reach, held_as=jnp.bfloat16):
    array = jax.random.normal(rng, shape, jnp.float32) * scale
    return jnp.minimum(jnp.maximum(array, -reach), reach).astype(held_as)


def setup_inputs(seed: int = 0) -> dict:
    keys = jax.random.split(jax.random.key(seed), 8)
    loader_rows = draw_loader_rows(jax.random.fold_in(keys[7], 71), 0)
    send_slot = draw_send_slot(jax.random.fold_in(keys[7], 71), 0)
    arrive_slot = draw_arrive_slot(jax.random.fold_in(keys[7], 71), 0)
    user_lengths = jax.vmap(lambda own: ragged_sizes(own, USERS, GROUP_ROWS, LONGEST, 2))(jax.random.split(keys[3], GROUPS)).reshape((GROUPS, USERS)).astype(jnp.int32)
    proj_weight = normal_values(keys[4], (D, 4 * D), D ** -0.5, 0.25)
    out_weight = normal_values(keys[5], (D, D), D ** -0.5, 0.25)
    cotangent = draw_cotangent(jax.random.fold_in(keys[7], 71), 0)
    return dict(loader_rows=loader_rows, send_slot=send_slot, arrive_slot=arrive_slot, user_lengths=user_lengths, proj_weight=proj_weight, out_weight=out_weight, cotangent=cotangent)


norm_eps = 1e-05

def normalize(values):
    centre = values - lax.optimization_barrier(jnp.mean(values, axis=-1, keepdims=True))
    inverse = lax.rsqrt(lax.optimization_barrier(jnp.mean(centre * centre, axis=-1, keepdims=True)) + norm_eps)
    return (centre * inverse, inverse)

def normalize_back(grad_in, normed, inverse):
    mean_grad = lax.optimization_barrier(jnp.mean(grad_in, axis=-1, keepdims=True))
    mean_cross = lax.optimization_barrier(jnp.mean(grad_in * normed, axis=-1, keepdims=True))
    return (grad_in - mean_grad - normed * mean_cross) * inverse

def silu_grad(values):
    sigma = jax.nn.sigmoid(values)
    return sigma * (1.0 + values * (1.0 - sigma))

def owner_rows(loader_rows, send_slot, arrive_slot):
    device_count = N_DP * N_CTX
    row_ids = jnp.arange(device_count * TOK_DEV, dtype=jnp.int32)
    home = (row_ids // TOK_DEV).astype(jnp.int32)
    within = (row_ids % TOK_DEV).astype(jnp.int32)
    table = jnp.zeros((device_count, device_count * CAP), jnp.int32).at[home, send_slot].set(within)
    source = (arrive_slot // CAP).astype(jnp.int32)
    place = (arrive_slot % CAP).astype(jnp.int32)
    picked = table[source, home * CAP + place]
    return loader_rows[source * TOK_DEV + picked]

def reference(loader_rows, send_slot, arrive_slot, user_lengths, proj_weight, out_weight, cotangent):
    owned = owner_rows(loader_rows, send_slot, arrive_slot).reshape(N_DP, GROUP_ROWS, D)
    cot_groups = cotangent.reshape(N_DP, GROUP_ROWS, D)
    head_dim = D // HEADS
    score_scale = head_dim ** (-0.5)
    row_index = jnp.arange(GROUP_ROWS, dtype=jnp.int32)
    half_rows = TOK_DEV // 2
    device_of = (row_index // TOK_DEV).astype(jnp.int32)
    local_of = (row_index % TOK_DEV).astype(jnp.int32)
    positions = jnp.where(local_of < half_rows, device_of * half_rows + local_of, GROUP_ROWS - (device_of + 1) * half_rows + (local_of - half_rows)).astype(jnp.int32)

    def split_heads(values):
        return values.reshape(GROUP_ROWS, HEADS, head_dim).transpose(1, 0, 2)

    def merge_heads(values):
        return values.transpose(1, 0, 2).reshape(GROUP_ROWS, D)

    def one_group(carry, inputs):
        rows, cot_rows, lengths = inputs
        ends = jnp.cumsum(lengths)
        users = lax.optimization_barrier(jnp.sum((ends[None, :] <= positions[:, None]).astype(jnp.int32), axis=1))
        allowed = (positions[None, :] <= positions[:, None]) & (users[:, None] == users[None, :])
        rows_f = rows.astype(jnp.float32)
        normed, inverse_in = normalize(rows_f)
        normed_bf = normed.astype(jnp.bfloat16)
        pre = jnp.dot(normed_bf, proj_weight, preferred_element_type=jnp.float32)
        proj = (pre * jax.nn.sigmoid(pre)).astype(jnp.bfloat16)
        update_rows = proj[:, :D]
        value_rows = proj[:, D:2 * D]
        query_rows = proj[:, 2 * D:3 * D]
        key_rows = proj[:, 3 * D:]
        heads_query = split_heads(query_rows)
        heads_key = split_heads(key_rows)
        heads_value = split_heads(value_rows)

        def head_forward(items):
            query_h, key_h, value_h = items
            scores = jnp.dot(query_h, key_h.T, preferred_element_type=jnp.float32) * score_scale
            weights = jnp.where(allowed, scores * jax.nn.sigmoid(scores), 0.0).astype(jnp.bfloat16)
            return jnp.dot(weights, value_h, preferred_element_type=jnp.float32)
        attended = merge_heads(lax.map(head_forward, (heads_query, heads_key, heads_value)))
        att_normed, inverse_att = normalize(attended)
        update_f = update_rows.astype(jnp.float32)
        gated = (att_normed * update_f).astype(jnp.bfloat16)
        layer_rows = (rows_f + jnp.dot(gated, out_weight, preferred_element_type=jnp.float32)).astype(jnp.bfloat16)
        out_term = jnp.dot(gated.T, cot_rows, preferred_element_type=jnp.float32)
        grad_gated = jnp.dot(cot_rows, out_weight.T, preferred_element_type=jnp.float32)
        grad_update = grad_gated * att_normed
        grad_att = normalize_back(grad_gated * update_f, att_normed, inverse_att).astype(jnp.bfloat16)

        def head_backward(items):
            query_h, key_h, value_h, grad_h = items
            scores = jnp.dot(query_h, key_h.T, preferred_element_type=jnp.float32) * score_scale
            weights = jnp.where(allowed, scores * jax.nn.sigmoid(scores), 0.0).astype(jnp.bfloat16)
            grad_weights = jnp.dot(grad_h, value_h.T, preferred_element_type=jnp.float32)
            grad_scores = jnp.where(allowed, grad_weights * silu_grad(scores) * score_scale, 0.0).astype(jnp.bfloat16)
            grad_q = jnp.dot(grad_scores, key_h, preferred_element_type=jnp.float32)
            grad_k = jnp.dot(grad_scores.T, query_h, preferred_element_type=jnp.float32)
            grad_v = jnp.dot(weights.T, grad_h, preferred_element_type=jnp.float32)
            return (grad_q, grad_k, grad_v)
        grad_q, grad_k, grad_v = lax.map(head_backward, (heads_query, heads_key, heads_value, split_heads(grad_att)))
        grad_proj = jnp.concatenate([grad_update, merge_heads(grad_v), merge_heads(grad_q), merge_heads(grad_k)], axis=1)
        grad_pre = (grad_proj * silu_grad(pre)).astype(jnp.bfloat16)
        proj_term = jnp.dot(normed_bf.T, grad_pre, preferred_element_type=jnp.float32)
        grad_normed = jnp.dot(grad_pre, proj_weight.T, preferred_element_type=jnp.float32)
        row_grads = (cot_rows.astype(jnp.float32) + normalize_back(grad_normed, normed, inverse_in)).astype(jnp.bfloat16)
        return ((carry[0] + proj_term, carry[1] + out_term), (layer_rows, row_grads))
    start_carry = (jnp.zeros((D, 4 * D), jnp.float32), jnp.zeros((D, D), jnp.float32))
    sums, outputs = lax.scan(one_group, start_carry, (owned, cot_groups, user_lengths))
    grad_scale = ALL_ROWS ** (-0.5)
    layer_out = outputs[0].reshape(ALL_ROWS, D)
    row_grads = outputs[1].reshape(ALL_ROWS, D)
    return (layer_out, row_grads, sums[0] * grad_scale, sums[1] * grad_scale)
```

```python
import functools

import jax
import jax.numpy as jnp
from jax import lax
from jax.experimental import pallas as pl
from jax.experimental.pallas import tpu as pltpu
from jax.sharding import PartitionSpec as P

HEADS = 8
EPS = 1e-05
TILE = 256
BF = jnp.bfloat16
F32 = jnp.float32
SRC_SHIFT = 16


def bits_of(count):
    return [1 << each for each in range(count.bit_length() - 1)]


def reverse_bits(value, count):
    width = count.bit_length() - 1
    result = 0
    for each in range(width):
        result = result | (((value >> each) & 1) << (width - 1 - each))
    return result


def swap(values, axis, distance):
    size = lax.axis_size(axis)
    return lax.ppermute(values, axis, [(each, each ^ distance) for each in range(size)])


def spread(values, axis, order):
    held = {0: values}
    for bit in order:
        held.update({key | bit: swap(held[key], axis, bit) for key in sorted(held)})
    return held


def nt_dot(left, right):
    return lax.dot_general(left, right, (((1,), (1,)), ((), ())), preferred_element_type=F32)


def tn_dot(left, right):
    return lax.dot_general(left, right, (((0,), (0,)), ((), ())), preferred_element_type=F32)


def nn_dot(left, right):
    return jnp.dot(left, right, preferred_element_type=F32)


def normalize(values):
    centre = values - jnp.mean(values, axis=-1, keepdims=True)
    inverse = lax.rsqrt(jnp.mean(centre * centre, axis=-1, keepdims=True) + EPS)
    return centre * inverse, inverse


def silu(values):
    half = 0.5 * values
    return half + half * jnp.tanh(half)


def silu_grad(values):
    half = 0.5 * values
    tanh = jnp.tanh(half)
    return (0.5 + 0.5 * tanh) * (1.0 + half * (1.0 - tanh))


def call(kernel, out_shapes, args, flops, smem=()):
    moved = sum(each.size * each.dtype.itemsize for each in list(args) + list(out_shapes))
    specs = [
        pl.BlockSpec(memory_space=pltpu.SMEM if index in smem else pltpu.VMEM)
        for index in range(len(args))
    ]
    return functools.partial(
        pl.pallas_call,
        kernel,
        out_shape=tuple(out_shapes),
        in_specs=specs,
        out_specs=tuple(pl.BlockSpec(memory_space=pltpu.VMEM) for _ in out_shapes),
        compiler_params=pltpu.CompilerParams(vmem_limit_bytes=50 * 1024 * 1024),
        cost_estimate=pl.CostEstimate(flops=flops, bytes_accessed=moved, transcendentals=0),
    )


def local(loader_rows, send_slot, arrive_slot, user_lengths, proj_weight, out_weight, cotangent):
    own_count = send_slot.shape[0]
    width = out_weight.shape[0]
    users = user_lengths.shape[1]
    ctx = lax.axis_size("ctx")
    dps = lax.axis_size("dp")
    devices = ctx * dps
    per_pair = own_count // devices
    cap = per_pair + max(1, per_pair // 2)
    half = own_count // 2
    rows_all = ctx * own_count
    blocks = 2 * ctx
    part = width // ctx
    heads = HEADS // ctx
    head_dim = width // HEADS
    scale = head_dim ** (-0.5)
    pair_rows = ctx * cap
    side_rows = dps // 2 * pair_rows
    tiles = rows_all // TILE
    ctx_bits = bits_of(ctx)
    me_ctx = lax.axis_index("ctx")
    me_dp = lax.axis_index("dp")
    shape = jax.ShapeDtypeStruct

    def block_of(device, side):
        return device if side == 0 else blocks - 1 - device

    def block_rows(device, side):
        return pl.ds(pl.multiple_of(block_of(device, side) * half, half), half)

    def pack_kernel(slot_ref, rows_ref, *out_refs):
        mine = lax.axis_index("dp")
        slots = slot_ref[...]
        rows = rows_ref[...]
        row_id = lax.broadcasted_iota(jnp.int32, (pair_rows, own_count), 0)
        for rel in range(dps):
            picked = (row_id + (mine ^ rel) * pair_rows == slots).astype(BF)
            out_refs[rel][...] = nn_dot(picked, rows).astype(BF)

    pack_args = (send_slot.reshape(1, own_count), loader_rows)
    pack_outs = [shape((pair_rows, width), BF)] * dps
    sent = call(pack_kernel, pack_outs, pack_args, 2 * dps * pair_rows * own_count * width)()(*pack_args)

    source = arrive_slot // cap
    place = arrive_slot % cap
    where_own = ((source % ctx) << SRC_SHIFT) + (
        ((source // ctx) ^ me_dp) * pair_rows + me_ctx * cap + place
    )
    where_of = spread(where_own.reshape(2, half), "ctx", ctx_bits)

    landed = [sent[0]] + [swap(sent[rel], "dp", rel) for rel in range(1, dps)]
    cot_of = spread(cotangent, "ctx", ctx_bits)
    sides = (
        spread(jnp.concatenate(landed[: dps // 2]), "ctx", ctx_bits),
        spread(jnp.concatenate(landed[dps // 2 :]), "ctx", ctx_bits[::-1]),
    )
    proj_own = lax.dynamic_index_in_dim(
        proj_weight.reshape(width, 4, ctx, part), me_ctx, 2, keepdims=False
    ).reshape(width, 4 * part)
    out_own = lax.dynamic_slice_in_dim(out_weight, me_ctx * part, part, 0)

    def gate_kernel(*refs):
        cot_refs, (weight_ref, grad_ref, cot_ref) = refs[:ctx], refs[ctx:]
        mine = lax.axis_index("ctx")
        for rel in range(ctx):
            for side in range(2):
                to = block_rows(mine ^ rel, side)
                piece = cot_refs[rel][side * half : (side + 1) * half, :]
                cot_ref[to, :] = piece
                grad_ref[to, :] = nt_dot(piece, weight_ref[...])

    gate_args = tuple(cot_of[rel] for rel in range(ctx)) + (out_own,)
    gate_outs = [shape((rows_all, part), F32), shape((rows_all, width), BF)]
    grad_gated, cot_all = call(gate_kernel, gate_outs, gate_args, 2 * rows_all * width * part)()(*gate_args)

    def start_of(positions, lengths_ref):
        end = 0
        begin = jnp.zeros_like(positions)
        for each in range(users):
            length = lengths_ref[0, each]
            end = end + length
            begin = begin + jnp.where(positions >= end, length, 0)
        return begin

    def lane_masks():
        lane = lax.broadcasted_iota(jnp.int32, (1, part), 1)
        return [
            (lane >= each * head_dim) & (lane < (each + 1) * head_dim) for each in range(heads)
        ]

    def forward_kernel(*refs):
        side_refs = (refs[:ctx], refs[ctx : 2 * ctx])
        where_refs = refs[2 * ctx : 3 * ctx]
        lengths_ref, weight_ref, gg_ref = refs[3 * ctx : 3 * ctx + 3]
        own_ref, norm_t_ref, pre_ref, proj_ref, att_ref, stat_ref = refs[3 * ctx + 3 : 3 * ctx + 9]
        where_ref, rows_ref, query_ref, value_ref = refs[3 * ctx + 9 :]
        mine = lax.axis_index("ctx")
        for rel in range(ctx):
            column = jnp.transpose(
                jnp.broadcast_to(where_refs[rel][...][:, None, :], (2, 8, half)).reshape(16, half)
            )
            for side in range(2):
                where_ref[block_rows(mine ^ rel, side), :] = column[:, side * 8 : side * 8 + 1]
        masks = lane_masks()
        source_row = lax.broadcasted_iota(jnp.int32, (TILE, side_rows), 1)
        for tile in range(tiles):
            span = pl.ds(tile * TILE, TILE)
            wanted = where_ref[span, :]
            total = jnp.zeros((TILE, width), F32)
            for rel in range(ctx):
                for side in range(2):
                    key = source_row + (((mine ^ rel) << SRC_SHIFT) + side * side_rows)
                    picked = (key == wanted).astype(BF)
                    total = total + nn_dot(picked, side_refs[side][rel][...])
            rows_ref[span, :] = total.astype(BF)
            normed = normalize(total)[0].astype(BF)
            norm_t_ref[:, tile * TILE : (tile + 1) * TILE] = jnp.transpose(normed)
            pre = nn_dot(normed, weight_ref[...])
            pre_ref[span, :] = pre
            proj = silu(pre).astype(BF)
            proj_ref[span, :] = proj
            query = proj[:, 2 * part : 3 * part] * jnp.asarray(0.5 * scale, BF)
            value = proj[:, part : 2 * part]
            for head in range(heads):
                query_ref[head, span, :] = jnp.where(masks[head], query, jnp.zeros_like(query))
                value_ref[head, span, :] = jnp.where(masks[head], value, jnp.zeros_like(value))
        for side in range(2):
            own_ref[side * half : (side + 1) * half, :] = rows_ref[block_rows(mine, side), :]
        for at in range(tiles):
            span = pl.ds(at * TILE, TILE)
            query_pos = lax.broadcasted_iota(jnp.int32, (TILE, 1), 0) + at * TILE
            begin = start_of(query_pos, lengths_ref)
            total = jnp.zeros((TILE, part), F32)
            for key_at in range(at + 1):
                key_span = pl.ds(key_at * TILE, TILE)
                key_pos = lax.broadcasted_iota(jnp.int32, (1, TILE), 1) + key_at * TILE
                allowed = key_pos >= begin
                if key_at == at:
                    allowed = allowed & (key_pos <= query_pos)
                key = proj_ref[key_span, 3 * part :]
                for head in range(heads):
                    score = nt_dot(query_ref[head, span, :], key)
                    weight = jnp.where(allowed, score + score * jnp.tanh(score), 0.0).astype(BF)
                    total = total + nn_dot(weight, value_ref[head, key_span, :])
            att_ref[span, :] = total
            grad = gg_ref[span, :] * proj_ref[span, :part].astype(F32)
            mean = jnp.mean(total, axis=-1, keepdims=True)
            centre = total - mean
            spread_sum = jnp.sum(centre * centre, axis=-1, keepdims=True)
            grad_sum = jnp.sum(grad, axis=-1, keepdims=True)
            cross_sum = jnp.sum(grad * centre, axis=-1, keepdims=True)
            lane = lax.broadcasted_iota(jnp.int32, (TILE, 128), 1)
            table = jnp.where(
                lane == 0, mean, jnp.where(lane == 1, spread_sum, jnp.where(lane == 2, grad_sum, cross_sum))
            )
            for sub in range(TILE // half):
                turned = jnp.transpose(table[sub * half : (sub + 1) * half, :])
                block = at * (TILE // half) + sub
                for each in range(4):
                    stat_ref[each, block : block + 1, :] = turned[each : each + 1, :]

    fwd_args = (
        tuple(sides[0][rel] for rel in range(ctx))
        + tuple(sides[1][rel] for rel in range(ctx))
        + tuple(where_of[rel] for rel in range(ctx))
        + (user_lengths, proj_own, grad_gated)
    )
    fwd_outs = [
        shape((own_count, width), BF),
        shape((width, rows_all), BF),
        shape((rows_all, 4 * part), F32),
        shape((rows_all, 4 * part), BF),
        shape((rows_all, part), F32),
        shape((4, blocks, half), F32),
    ]
    own_rows, norm_t, pre, proj, attended, stats = call(
        forward_kernel, fwd_outs, fwd_args, 4 * rows_all * rows_all * part, smem=(3 * ctx,)
    )(
        scratch_shapes=[
            pltpu.VMEM((rows_all, 1), jnp.int32),
            pltpu.VMEM((rows_all, width), BF),
            pltpu.VMEM((heads, rows_all, part), BF),
            pltpu.VMEM((heads, rows_all, part), BF),
        ]
    )(*fwd_args)

    stats_of = [stats] + [swap(stats, "ctx", rel) for rel in range(1, ctx)]

    def slot_of(index):
        return reverse_bits(index ^ lax.axis_index("dp"), dps)

    def middle_kernel(*refs):
        stat_refs = refs[:ctx]
        att_ref, gg_ref, update_ref, pre_ref, norm_t_ref, cot_ref = refs[ctx : ctx + 6]
        gated_refs = refs[ctx + 6 : 2 * ctx + 6]
        grad_att_ref, grad_pre_ref, proj_ref, out_ref = refs[2 * ctx + 6 : 2 * ctx + 10]
        gated_ref = refs[2 * ctx + 10]
        mine = lax.axis_index("ctx")
        means = [each[0] for each in stat_refs]
        mean = sum(means) / ctx
        spread_sum = sum(each[1] + part * (own - mean) ** 2 for each, own in zip(stat_refs, means))
        inverse = lax.rsqrt(spread_sum / width + EPS)
        grad_mean = sum(each[2] for each in stat_refs) / width
        cross = sum(each[3] + each[2] * (own - mean) for each, own in zip(stat_refs, means))
        cross_mean = inverse * cross / width
        for block in range(blocks):
            span = pl.ds(block * half, half)
            table = jnp.concatenate(
                [each[block : block + 1, :] for each in (mean, inverse, grad_mean, cross_mean)] * 2
            )
            columns = jnp.transpose(table)
            mean_c, inverse_c, grad_c, cross_c = (columns[:, each : each + 1] for each in range(4))
            normed = (att_ref[span, :] - mean_c) * inverse_c
            grad = gg_ref[span, :]
            update = update_ref[span, :].astype(F32)
            gated_ref[span, :] = (normed * update).astype(BF)
            grad_att_ref[span, :] = ((grad * update - grad_c - normed * cross_c) * inverse_c).astype(BF)
            grad_pre_ref[span, :] = (grad * normed * silu_grad(pre_ref[span, :])).astype(BF)
        for rel in range(ctx):
            for side in range(2):
                gated_refs[rel][side * half : (side + 1) * half, :] = gated_ref[
                    block_rows(mine ^ rel, side), :
                ]
        proj_ref[...] = nn_dot(norm_t_ref[...], grad_pre_ref[...]).astype(BF)
        out_ref[...] = tn_dot(gated_ref[...], cot_ref[...]).astype(BF)

    mid_args = tuple(stats_of) + (
        attended,
        grad_gated,
        proj[:, :part],
        pre[:, :part],
        norm_t,
        cot_all,
    )
    mid_outs = [shape((own_count, part), BF)] * ctx + [
        shape((rows_all, part), BF),
        shape((rows_all, part), BF),
        shape((width, part), BF),
        shape((part, width), BF),
    ]
    results = call(middle_kernel, mid_outs, mid_args, 4 * rows_all * part * width)(
        scratch_shapes=[pltpu.VMEM((rows_all, part), BF)]
    )(*mid_args)
    gated_parts, (grad_att, grad_update, proj_early, out_early) = results[:ctx], results[ctx:]
    gated_own = [gated_parts[0]] + [swap(gated_parts[rel], "ctx", rel) for rel in range(1, ctx)]

    order = (ctx_bits, ctx_bits[::-1])

    def backward_kernel(lengths_ref, weight_ref, proj_ref, pre_ref, norm_t_ref, grad_att_ref, grad_u_ref, *refs):
        late_ref, dn_refs = refs[0], (refs[1:3], refs[3:5])
        query_ref, key_ref, grad_ref, dq_ref, gp_ref = refs[5:]
        mine = lax.axis_index("ctx")
        masks = lane_masks()

        def masked(values, head):
            return jnp.where(masks[head], values, jnp.zeros_like(values))

        for tile in range(tiles):
            span = pl.ds(tile * TILE, TILE)
            for head in range(heads):
                query_ref[head, span, :] = masked(
                    proj_ref[span, 2 * part : 3 * part] * jnp.asarray(0.5 * scale, BF), head
                )
                key_ref[head, span, :] = masked(proj_ref[span, 3 * part :], head)
                grad_ref[head, span, :] = masked(grad_att_ref[span, :], head)
            gp_ref[span, :part] = grad_u_ref[span, :]
            dq_ref[span, :] = jnp.zeros((TILE, part), F32)
        for key_at in range(tiles):
            key_span = pl.ds(key_at * TILE, TILE)
            key_pos = lax.broadcasted_iota(jnp.int32, (TILE, 1), 0) + key_at * TILE
            key = proj_ref[key_span, 3 * part :]
            value = proj_ref[key_span, part : 2 * part] * jnp.asarray(0.5 * scale, BF)
            grad_key = jnp.zeros((TILE, part), F32)
            grad_value = jnp.zeros((TILE, part), F32)
            for at in range(key_at, tiles):
                span = pl.ds(at * TILE, TILE)
                query_pos = lax.broadcasted_iota(jnp.int32, (1, TILE), 1) + at * TILE
                allowed = key_pos >= start_of(query_pos, lengths_ref)
                if at == key_at:
                    allowed = allowed & (key_pos <= query_pos)
                grad_query = jnp.zeros((TILE, part), F32)
                for head in range(heads):
                    score = nt_dot(key, query_ref[head, span, :])
                    tanh = jnp.tanh(score)
                    cross = score * tanh
                    weight = jnp.where(allowed, score + cross, 0.0).astype(BF)
                    grad_value = grad_value + nn_dot(weight, grad_ref[head, span, :])
                    grad_weight = nt_dot(value, grad_ref[head, span, :])
                    slope = (1.0 + tanh) * (1.0 + score - cross)
                    grad_score = jnp.where(allowed, grad_weight * slope, 0.0).astype(BF)
                    grad_key = grad_key + nn_dot(grad_score, query_ref[head, span, :])
                    grad_query = grad_query + tn_dot(grad_score, key_ref[head, key_span, :])
                dq_ref[span, :] = dq_ref[span, :] + grad_query
            gp_ref[key_span, part : 2 * part] = (
                grad_value * silu_grad(pre_ref[key_span, part : 2 * part])
            ).astype(BF)
            gp_ref[key_span, 3 * part :] = (
                grad_key * (2.0 / scale) * silu_grad(pre_ref[key_span, 3 * part :])
            ).astype(BF)
        for tile in range(tiles):
            span = pl.ds(tile * TILE, TILE)
            gp_ref[span, 2 * part : 3 * part] = (
                dq_ref[span, :] * silu_grad(pre_ref[span, 2 * part : 3 * part])
            ).astype(BF)
        for side in range(2):
            for slot in range(ctx):
                rel = reverse_bits(slot, ctx) if side == 0 else slot
                piece = nt_dot(gp_ref[block_rows(mine ^ rel, side), :], weight_ref[...]).astype(BF)
                dn_refs[side][slot // (ctx // 2)][slot % (ctx // 2)] = piece
        late_ref[...] = nn_dot(norm_t_ref[...], gp_ref[:, part:]).astype(BF)

    bwd_args = (user_lengths, proj_own, proj, pre, norm_t, grad_att, grad_update)
    bwd_outs = [shape((width, 3 * part), BF)] + [shape((ctx // 2, half, width), BF)] * 4
    late, *dn_parts = call(
        backward_kernel, bwd_outs, bwd_args, 10 * rows_all * rows_all * part, smem=(0,)
    )(
        scratch_shapes=[
            pltpu.VMEM((heads, rows_all, part), BF),
            pltpu.VMEM((heads, rows_all, part), BF),
            pltpu.VMEM((heads, rows_all, part), BF),
            pltpu.VMEM((rows_all, part), F32),
            pltpu.VMEM((rows_all, 4 * part), BF),
        ]
    )(*bwd_args)

    dn_own = []
    for side in range(2):
        keep, send = dn_parts[2 * side : 2 * side + 2]
        for step, bit in enumerate(order[side]):
            got = swap(send, "ctx", bit)
            if step + 1 < len(order[side]):
                count = keep.shape[0] // 2
                total = keep.astype(F32) + got.astype(F32)
                keep, send = total[:count].astype(BF), total[count:].astype(BF)
        dn_own += [keep[0], got[0]]

    def layer_kernel(*refs):
        mine = lax.axis_index("ctx")
        total = refs[ctx][...].astype(F32)
        for rel in range(ctx):
            at = pl.ds(pl.multiple_of((mine ^ rel) * part, part), part)
            total = total + nn_dot(refs[rel][...], refs[ctx + 1][at, :])
        refs[ctx + 2][...] = total.astype(BF)

    layer_args = tuple(gated_own) + (own_rows, out_weight)
    (layer_out,) = call(
        layer_kernel, [shape((own_count, width), BF)], layer_args, 2 * own_count * width * width
    )()(*layer_args)

    def rows_kernel(keep_a, got_a, keep_b, got_b, rows_ref, cot_ref, out_ref):
        for side, (keep, got) in enumerate(((keep_a, got_a), (keep_b, got_b))):
            at = slice(side * half, (side + 1) * half)
            grad = keep[...].astype(F32) + got[...].astype(F32)
            normed, inverse = normalize(rows_ref[at, :].astype(F32))
            mean_grad = jnp.mean(grad, axis=-1, keepdims=True)
            mean_cross = jnp.mean(grad * normed, axis=-1, keepdims=True)
            back = (grad - mean_grad - normed * mean_cross) * inverse
            out_ref[at, :] = (cot_ref[at, :].astype(F32) + back).astype(BF)

    rows_args = tuple(dn_own) + (own_rows, cotangent)
    (row_grads,) = call(
        rows_kernel, [shape((own_count, width), BF)], rows_args, own_count * width * 20
    )()(*rows_args)

    dp_bits = bits_of(dps)
    proj_step, out_step = width // dps, part // dps
    rev = jnp.array([reverse_bits(each, dps) for each in range(dps)], jnp.int32)

    def by_slot(values):
        return jnp.take(values, rev ^ me_dp, axis=0)

    early_pieces = jnp.concatenate(
        [
            proj_early.reshape(dps, proj_step, part),
            out_early.reshape(dps, out_step, ctx, part).transpose(0, 2, 1, 3).reshape(dps, ctx * out_step, part),
        ],
        axis=1,
    )
    late_pieces = late.reshape(dps, proj_step, 3 * part)

    def reduce_dp(pieces):
        for bit in dp_bits:
            count = pieces.shape[0] // 2
            got = swap(pieces[count:], "dp", bit)
            pieces = (pieces[:count].astype(F32) + got.astype(F32)).astype(BF)
        return pieces

    def gather_all(piece):
        first = {0: piece}
        held = piece
        keys = [0]
        for bit in dp_bits[:1:-1]:
            held = jnp.concatenate([held, swap(held, "dp", bit)])
            keys = keys + [key | bit for key in keys]
        last = dp_bits[1]
        pair = (held, swap(held, "dp", last))
        out = {}
        for side in range(2):
            for rel, values in spread(pair[side], "ctx", order[side]).items():
                other = swap(values, "dp", 1)
                for at, key in enumerate(keys):
                    out[rel, key | (last * side)] = values[at]
                    out[rel, key | (last * side) | 1] = other[at]
        return out

    early_all = gather_all(reduce_dp(by_slot(early_pieces)))
    late_all = gather_all(reduce_dp(by_slot(late_pieces)))
    grad_scale = (own_count * devices) ** (-0.5)

    def absolute(pieces):
        table = jnp.stack([jnp.stack([pieces[c, d] for d in range(dps)]) for c in range(ctx)])
        table = jnp.take(table, jnp.arange(ctx) ^ me_ctx, axis=0)
        return jnp.take(table, jnp.arange(dps) ^ me_dp, axis=1)

    early_abs = absolute(early_all)
    late_abs = absolute(late_all)
    proj_u = early_abs[:, :, :proj_step, None, :]
    proj_rest = late_abs.reshape(ctx, dps, proj_step, 3, part)
    proj_grad = (
        jnp.concatenate([proj_u, proj_rest], axis=3)
        .transpose(1, 2, 3, 0, 4)
        .reshape(width, 4 * width)
        .astype(F32)
        * grad_scale
    )
    out_grad = (
        early_abs[:, :, proj_step:, :]
        .reshape(ctx, dps, ctx, out_step, part)
        .transpose(0, 1, 3, 2, 4)
        .reshape(width, width)
        .astype(F32)
        * grad_scale
    )
    return (layer_out, row_grads, proj_grad, out_grad)


def solution(mesh):
    placed = (
        P(("dp", "ctx"), None),
        P(("dp", "ctx")),
        P(("dp", "ctx")),
        P("dp", None),
        P(),
        P(),
        P(("dp", "ctx"), None),
    )
    return jax.shard_map(
        local,
        mesh=mesh,
        in_specs=placed,
        out_specs=(P(("dp", "ctx"), None), P(("dp", "ctx"), None), P(), P()),
        check_vma=False,
    )
```

```python
import functools

import jax
import jax.numpy as jnp
from jax import lax
from jax.experimental import pallas as pl
from jax.experimental.pallas import tpu as pltpu
from jax.sharding import PartitionSpec as P

HEADS = 8
EPS = 1e-05
TILE = 256
BF = jnp.bfloat16
F32 = jnp.float32
SRC_SHIFT = 16


def bits_of(count):
    return [1 << each for each in range(count.bit_length() - 1)]


def reverse_bits(value, count):
    width = count.bit_length() - 1
    result = 0
    for each in range(width):
        result = result | (((value >> each) & 1) << (width - 1 - each))
    return result


def swap(values, axis, distance):
    size = lax.axis_size(axis)
    return lax.ppermute(values, axis, [(each, each ^ distance) for each in range(size)])


def spread(values, axis, order):
    held = {0: values}
    for bit in order:
        held.update({key | bit: swap(held[key], axis, bit) for key in sorted(held)})
    return held


def nt_dot(left, right):
    return lax.dot_general(left, right, (((1,), (1,)), ((), ())), preferred_element_type=F32)


def tn_dot(left, right):
    return lax.dot_general(left, right, (((0,), (0,)), ((), ())), preferred_element_type=F32)


def nn_dot(left, right):
    return jnp.dot(left, right, preferred_element_type=F32)


def normalize(values):
    centre = values - jnp.mean(values, axis=-1, keepdims=True)
    inverse = lax.rsqrt(jnp.mean(centre * centre, axis=-1, keepdims=True) + EPS)
    return centre * inverse, inverse


def silu(values):
    half = 0.5 * values
    return half + half * jnp.tanh(half)


def silu_grad(values):
    half = 0.5 * values
    tanh = jnp.tanh(half)
    return (0.5 + 0.5 * tanh) * (1.0 + half * (1.0 - tanh))


def call(kernel, out_shapes, args, flops, smem=()):
    moved = sum(each.size * each.dtype.itemsize for each in list(args) + list(out_shapes))
    specs = [
        pl.BlockSpec(memory_space=pltpu.SMEM if index in smem else pltpu.VMEM)
        for index in range(len(args))
    ]
    return functools.partial(
        pl.pallas_call,
        kernel,
        out_shape=tuple(out_shapes),
        in_specs=specs,
        out_specs=tuple(pl.BlockSpec(memory_space=pltpu.VMEM) for _ in out_shapes),
        compiler_params=pltpu.CompilerParams(vmem_limit_bytes=50 * 1024 * 1024),
        cost_estimate=pl.CostEstimate(flops=flops, bytes_accessed=moved, transcendentals=0),
    )


def local(loader_rows, send_slot, arrive_slot, user_lengths, proj_weight, out_weight, cotangent):
    own_count = send_slot.shape[0]
    width = out_weight.shape[0]
    users = user_lengths.shape[1]
    ctx = lax.axis_size("ctx")
    dps = lax.axis_size("dp")
    devices = ctx * dps
    per_pair = own_count // devices
    cap = per_pair + max(1, per_pair // 2)
    half = own_count // 2
    rows_all = ctx * own_count
    blocks = 2 * ctx
    part = width // ctx
    heads = HEADS // ctx
    head_dim = width // HEADS
    scale = head_dim ** (-0.5)
    pair_rows = ctx * cap
    side_rows = dps // 2 * pair_rows
    tiles = rows_all // TILE
    ctx_bits = bits_of(ctx)
    me_ctx = lax.axis_index("ctx")
    me_dp = lax.axis_index("dp")
    shape = jax.ShapeDtypeStruct
    dp_bits = bits_of(dps)
    proj_step, out_step = width // dps, part // dps
    early_rows, late_rows = proj_step + ctx * out_step, 3 * proj_step
    packed = part % 128 == 0 and out_step % 16 == 0
    grad_scale = (own_count * devices) ** (-0.5)

    def block_of(device, side):
        return device if side == 0 else blocks - 1 - device

    def block_rows(device, side):
        return pl.ds(pl.multiple_of(block_of(device, side) * half, half), half)

    def pack_kernel(slot_ref, rows_ref, *out_refs):
        mine = lax.axis_index("dp")
        slots = slot_ref[...]
        rows = rows_ref[...]
        row_id = lax.broadcasted_iota(jnp.int32, (pair_rows, own_count), 0)
        for rel in range(dps):
            picked = (row_id + (mine ^ rel) * pair_rows == slots).astype(BF)
            out_refs[rel][...] = nn_dot(picked, rows).astype(BF)

    pack_args = (send_slot.reshape(1, own_count), loader_rows)
    pack_outs = [shape((pair_rows, width), BF)] * dps
    sent = call(pack_kernel, pack_outs, pack_args, 2 * dps * pair_rows * own_count * width)()(*pack_args)

    source = arrive_slot // cap
    place = arrive_slot % cap
    where_own = ((source % ctx) << SRC_SHIFT) + (
        ((source // ctx) ^ me_dp) * pair_rows + me_ctx * cap + place
    )
    where_of = spread(where_own.reshape(2, half), "ctx", ctx_bits)

    landed = [sent[0]] + [swap(sent[rel], "dp", rel) for rel in range(1, dps)]
    cot_of = spread(cotangent, "ctx", ctx_bits)
    sides = (
        spread(jnp.concatenate(landed[: dps // 2]), "ctx", ctx_bits),
        spread(jnp.concatenate(landed[dps // 2 :]), "ctx", ctx_bits[::-1]),
    )
    proj_own = jnp.concatenate(
        [
            lax.dynamic_slice_in_dim(proj_weight, each * width + me_ctx * part, part, 1)
            for each in range(4)
        ],
        axis=1,
    )
    out_own = lax.dynamic_slice_in_dim(out_weight, me_ctx * part, part, 0)

    def gate_kernel(*refs):
        cot_refs, (weight_ref, grad_ref, cot_ref) = refs[:ctx], refs[ctx:]
        mine = lax.axis_index("ctx")
        for rel in range(ctx):
            for side in range(2):
                to = block_rows(mine ^ rel, side)
                piece = cot_refs[rel][side * half : (side + 1) * half, :]
                cot_ref[to, :] = piece
                grad_ref[to, :] = nt_dot(piece, weight_ref[...])

    gate_args = tuple(cot_of[rel] for rel in range(ctx)) + (out_own,)
    gate_outs = [shape((rows_all, part), F32), shape((rows_all, width), BF)]
    grad_gated, cot_all = call(gate_kernel, gate_outs, gate_args, 2 * rows_all * width * part)()(*gate_args)

    def start_of(positions, lengths_ref):
        end = 0
        begin = jnp.zeros_like(positions)
        for each in range(users):
            length = lengths_ref[0, each]
            end = end + length
            begin = begin + jnp.where(positions >= end, length, 0)
        return begin

    def lane_masks():
        lane = lax.broadcasted_iota(jnp.int32, (1, part), 1)
        return [
            (lane >= each * head_dim) & (lane < (each + 1) * head_dim) for each in range(heads)
        ]

    def forward_kernel(*refs):
        side_refs = (refs[:ctx], refs[ctx : 2 * ctx])
        where_refs = refs[2 * ctx : 3 * ctx]
        lengths_ref, weight_ref, gg_ref = refs[3 * ctx : 3 * ctx + 3]
        own_ref, norm_t_ref, pre_ref, proj_ref, att_ref, stat_ref = refs[3 * ctx + 3 : 3 * ctx + 9]
        where_ref, rows_ref, query_ref, value_ref = refs[3 * ctx + 9 :]
        mine = lax.axis_index("ctx")
        for rel in range(ctx):
            column = jnp.transpose(
                jnp.broadcast_to(where_refs[rel][...][:, None, :], (2, 8, half)).reshape(16, half)
            )
            for side in range(2):
                where_ref[block_rows(mine ^ rel, side), :] = column[:, side * 8 : side * 8 + 1]
        masks = lane_masks()
        source_row = lax.broadcasted_iota(jnp.int32, (TILE, side_rows), 1)
        for tile in range(tiles):
            span = pl.ds(tile * TILE, TILE)
            wanted = where_ref[span, :]
            total = jnp.zeros((TILE, width), F32)
            for rel in range(ctx):
                for side in range(2):
                    key = source_row + (((mine ^ rel) << SRC_SHIFT) + side * side_rows)
                    picked = (key == wanted).astype(BF)
                    total = total + nn_dot(picked, side_refs[side][rel][...])
            rows_ref[span, :] = total.astype(BF)
            normed = normalize(total)[0].astype(BF)
            norm_t_ref[:, tile * TILE : (tile + 1) * TILE] = jnp.transpose(normed)
            pre = nn_dot(normed, weight_ref[...])
            pre_ref[span, :] = pre
            proj = silu(pre).astype(BF)
            proj_ref[span, :] = proj
            query = proj[:, 2 * part : 3 * part] * jnp.asarray(0.5 * scale, BF)
            value = proj[:, part : 2 * part]
            for head in range(heads):
                query_ref[head, span, :] = jnp.where(masks[head], query, jnp.zeros_like(query))
                value_ref[head, span, :] = jnp.where(masks[head], value, jnp.zeros_like(value))
        for side in range(2):
            own_ref[side * half : (side + 1) * half, :] = rows_ref[block_rows(mine, side), :]
        for at in range(tiles):
            span = pl.ds(at * TILE, TILE)
            query_pos = lax.broadcasted_iota(jnp.int32, (TILE, 1), 0) + at * TILE
            begin = start_of(query_pos, lengths_ref)
            total = jnp.zeros((TILE, part), F32)
            for key_at in range(at + 1):
                key_span = pl.ds(key_at * TILE, TILE)
                key_pos = lax.broadcasted_iota(jnp.int32, (1, TILE), 1) + key_at * TILE
                allowed = key_pos >= begin
                if key_at == at:
                    allowed = allowed & (key_pos <= query_pos)
                key = proj_ref[key_span, 3 * part :]
                for head in range(heads):
                    score = nt_dot(query_ref[head, span, :], key)
                    weight = jnp.where(allowed, score + score * jnp.tanh(score), 0.0).astype(BF)
                    total = total + nn_dot(weight, value_ref[head, key_span, :])
            att_ref[span, :] = total
            grad = gg_ref[span, :] * proj_ref[span, :part].astype(F32)
            mean = jnp.mean(total, axis=-1, keepdims=True)
            centre = total - mean
            spread_sum = jnp.sum(centre * centre, axis=-1, keepdims=True)
            grad_sum = jnp.sum(grad, axis=-1, keepdims=True)
            cross_sum = jnp.sum(grad * centre, axis=-1, keepdims=True)
            lane = lax.broadcasted_iota(jnp.int32, (TILE, 128), 1)
            table = jnp.where(
                lane == 0, mean, jnp.where(lane == 1, spread_sum, jnp.where(lane == 2, grad_sum, cross_sum))
            )
            for sub in range(TILE // half):
                turned = jnp.transpose(table[sub * half : (sub + 1) * half, :])
                block = at * (TILE // half) + sub
                for each in range(4):
                    stat_ref[each, block : block + 1, :] = turned[each : each + 1, :]

    fwd_args = (
        tuple(sides[0][rel] for rel in range(ctx))
        + tuple(sides[1][rel] for rel in range(ctx))
        + tuple(where_of[rel] for rel in range(ctx))
        + (user_lengths, proj_own, grad_gated)
    )
    fwd_outs = [
        shape((own_count, width), BF),
        shape((width, rows_all), BF),
        shape((rows_all, 4 * part), F32),
        shape((rows_all, 4 * part), BF),
        shape((rows_all, part), F32),
        shape((4, blocks, half), F32),
    ]
    own_rows, norm_t, pre, proj, attended, stats = call(
        forward_kernel, fwd_outs, fwd_args, 4 * rows_all * rows_all * part, smem=(3 * ctx,)
    )(
        scratch_shapes=[
            pltpu.VMEM((rows_all, 1), jnp.int32),
            pltpu.VMEM((rows_all, width), BF),
            pltpu.VMEM((heads, rows_all, part), BF),
            pltpu.VMEM((heads, rows_all, part), BF),
        ]
    )(*fwd_args)

    stats_of = [stats] + [swap(stats, "ctx", rel) for rel in range(1, ctx)]

    def slots(mine):
        return [(slot, reverse_bits(slot, dps) ^ mine) for slot in range(dps)]

    def middle_kernel(*refs):
        stat_refs = refs[:ctx]
        att_ref, gg_ref, update_ref, pre_ref, norm_t_ref, cot_ref = refs[ctx : ctx + 6]
        gated_refs = refs[ctx + 6 : 2 * ctx + 6]
        grad_att_ref, grad_pre_ref = refs[2 * ctx + 6 : 2 * ctx + 8]
        early_refs = refs[2 * ctx + 8 : 2 * ctx + 10]
        gated_ref, proj_ref, out_ref = refs[2 * ctx + 10 :]
        mine = lax.axis_index("ctx")
        means = [each[0] for each in stat_refs]
        mean = sum(means) / ctx
        spread_sum = sum(each[1] + part * (own - mean) ** 2 for each, own in zip(stat_refs, means))
        inverse = lax.rsqrt(spread_sum / width + EPS)
        grad_mean = sum(each[2] for each in stat_refs) / width
        cross = sum(each[3] + each[2] * (own - mean) for each, own in zip(stat_refs, means))
        cross_mean = inverse * cross / width
        for block in range(blocks):
            span = pl.ds(block * half, half)
            table = jnp.concatenate(
                [each[block : block + 1, :] for each in (mean, inverse, grad_mean, cross_mean)] * 2
            )
            columns = jnp.transpose(table)
            mean_c, inverse_c, grad_c, cross_c = (columns[:, each : each + 1] for each in range(4))
            normed = (att_ref[span, :] - mean_c) * inverse_c
            grad = gg_ref[span, :]
            update = update_ref[span, :].astype(F32)
            gated_ref[span, :] = (normed * update).astype(BF)
            grad_att_ref[span, :] = ((grad * update - grad_c - normed * cross_c) * inverse_c).astype(BF)
            grad_pre_ref[span, :] = (grad * normed * silu_grad(pre_ref[span, :])).astype(BF)
        for rel in range(ctx):
            for side in range(2):
                gated_refs[rel][side * half : (side + 1) * half, :] = gated_ref[
                    block_rows(mine ^ rel, side), :
                ]
        proj_ref[...] = nn_dot(norm_t_ref[...], grad_pre_ref[...]).astype(BF)
        out_ref[...] = tn_dot(gated_ref[...], cot_ref[...]).astype(BF)
        if not packed:
            early_refs[0][...] = proj_ref[...]
            early_refs[1][...] = out_ref[...]
            return
        for slot, index in slots(lax.axis_index("dp")):
            to = early_refs[slot // (dps // 2)].at[slot % (dps // 2)]
            to[:proj_step, :] = proj_ref[pl.ds(pl.multiple_of(index * proj_step, proj_step), proj_step), :]
            out_rows = pl.ds(pl.multiple_of(index * out_step, out_step), out_step)
            for each in range(ctx):
                first = proj_step + each * out_step
                to[first : first + out_step, :] = out_ref[out_rows, each * part : (each + 1) * part]

    mid_args = tuple(stats_of) + (
        attended,
        grad_gated,
        proj[:, :part],
        pre[:, :part],
        norm_t,
        cot_all,
    )
    mid_outs = [shape((own_count, part), BF)] * ctx + [
        shape((rows_all, part), BF),
        shape((rows_all, part), BF),
    ]
    if packed:
        mid_outs += [shape((dps // 2, early_rows, part), BF)] * 2
    else:
        mid_outs += [shape((width, part), BF), shape((part, width), BF)]
    results = call(middle_kernel, mid_outs, mid_args, 4 * rows_all * part * width)(
        scratch_shapes=[
            pltpu.VMEM((rows_all, part), BF),
            pltpu.VMEM((width, part), BF),
            pltpu.VMEM((part, width), BF),
        ]
    )(*mid_args)
    gated_parts, (grad_att, grad_update, *early_parts) = results[:ctx], results[ctx:]
    gated_own = [gated_parts[0]] + [swap(gated_parts[rel], "ctx", rel) for rel in range(1, ctx)]

    order = (ctx_bits, ctx_bits[::-1])

    def backward_kernel(lengths_ref, weight_ref, proj_ref, pre_ref, norm_t_ref, grad_att_ref, grad_u_ref, *refs):
        late_refs, dn_refs = refs[:2], (refs[2:4], refs[4:6])
        query_ref, key_ref, grad_ref, dq_ref, gp_ref, late_ref = refs[6:]
        mine = lax.axis_index("ctx")
        masks = lane_masks()

        def masked(values, head):
            return jnp.where(masks[head], values, jnp.zeros_like(values))

        for tile in range(tiles):
            span = pl.ds(tile * TILE, TILE)
            for head in range(heads):
                query_ref[head, span, :] = masked(
                    proj_ref[span, 2 * part : 3 * part] * jnp.asarray(0.5 * scale, BF), head
                )
                key_ref[head, span, :] = masked(proj_ref[span, 3 * part :], head)
                grad_ref[head, span, :] = masked(grad_att_ref[span, :], head)
            gp_ref[span, :part] = grad_u_ref[span, :]
            dq_ref[span, :] = jnp.zeros((TILE, part), F32)
        for key_at in range(tiles):
            key_span = pl.ds(key_at * TILE, TILE)
            key_pos = lax.broadcasted_iota(jnp.int32, (TILE, 1), 0) + key_at * TILE
            key = proj_ref[key_span, 3 * part :]
            value = proj_ref[key_span, part : 2 * part] * jnp.asarray(0.5 * scale, BF)
            grad_key = jnp.zeros((TILE, part), F32)
            grad_value = jnp.zeros((TILE, part), F32)
            for at in range(key_at, tiles):
                span = pl.ds(at * TILE, TILE)
                query_pos = lax.broadcasted_iota(jnp.int32, (1, TILE), 1) + at * TILE
                allowed = key_pos >= start_of(query_pos, lengths_ref)
                if at == key_at:
                    allowed = allowed & (key_pos <= query_pos)
                grad_query = jnp.zeros((TILE, part), F32)
                for head in range(heads):
                    score = nt_dot(key, query_ref[head, span, :])
                    tanh = jnp.tanh(score)
                    cross = score * tanh
                    weight = jnp.where(allowed, score + cross, 0.0).astype(BF)
                    grad_value = grad_value + nn_dot(weight, grad_ref[head, span, :])
                    grad_weight = nt_dot(value, grad_ref[head, span, :])
                    slope = (1.0 + tanh) * (1.0 + score - cross)
                    grad_score = jnp.where(allowed, grad_weight * slope, 0.0).astype(BF)
                    grad_key = grad_key + nn_dot(grad_score, query_ref[head, span, :])
                    grad_query = grad_query + tn_dot(grad_score, key_ref[head, key_span, :])
                dq_ref[span, :] = dq_ref[span, :] + grad_query
            gp_ref[key_span, part : 2 * part] = (
                grad_value * silu_grad(pre_ref[key_span, part : 2 * part])
            ).astype(BF)
            gp_ref[key_span, 3 * part :] = (
                grad_key * (2.0 / scale) * silu_grad(pre_ref[key_span, 3 * part :])
            ).astype(BF)
        for tile in range(tiles):
            span = pl.ds(tile * TILE, TILE)
            gp_ref[span, 2 * part : 3 * part] = (
                dq_ref[span, :] * silu_grad(pre_ref[span, 2 * part : 3 * part])
            ).astype(BF)
        late_ref[...] = nn_dot(norm_t_ref[...], gp_ref[:, part:]).astype(BF)
        if packed:
            for slot, index in slots(lax.axis_index("dp")):
                rows = pl.ds(pl.multiple_of(index * proj_step, proj_step), proj_step)
                for each in range(3):
                    late_refs[slot // (dps // 2)][
                        slot % (dps // 2), each * proj_step : (each + 1) * proj_step, :
                    ] = late_ref[rows, each * part : (each + 1) * part]
        else:
            late_refs[0][...] = late_ref[: width // 2, :]
            late_refs[1][...] = late_ref[width // 2 :, :]
        for side in range(2):
            for slot in range(ctx):
                rel = reverse_bits(slot, ctx) if side == 0 else slot
                piece = nt_dot(gp_ref[block_rows(mine ^ rel, side), :], weight_ref[...]).astype(BF)
                dn_refs[side][slot // (ctx // 2)][slot % (ctx // 2)] = piece

    bwd_args = (user_lengths, proj_own, proj, pre, norm_t, grad_att, grad_update)
    bwd_outs = [
        shape((dps // 2, late_rows, part) if packed else (width // 2, 3 * part), BF)
    ] * 2 + [shape((ctx // 2, half, width), BF)] * 4
    *late_parts, dn_a, dn_b, dn_c, dn_d = call(
        backward_kernel, bwd_outs, bwd_args, 10 * rows_all * rows_all * part, smem=(0,)
    )(
        scratch_shapes=[
            pltpu.VMEM((heads, rows_all, part), BF),
            pltpu.VMEM((heads, rows_all, part), BF),
            pltpu.VMEM((heads, rows_all, part), BF),
            pltpu.VMEM((rows_all, part), F32),
            pltpu.VMEM((rows_all, 4 * part), BF),
            pltpu.VMEM((width, 3 * part), BF),
        ]
    )(*bwd_args)
    dn_parts = (dn_a, dn_b, dn_c, dn_d)

    dn_own = []
    for side in range(2):
        keep, send = dn_parts[2 * side : 2 * side + 2]
        for step, bit in enumerate(order[side]):
            got = swap(send, "ctx", bit)
            if step + 1 < len(order[side]):
                count = keep.shape[0] // 2
                total = keep.astype(F32) + got.astype(F32)
                keep, send = total[:count].astype(BF), total[count:].astype(BF)
        dn_own += [keep[0], got[0]]

    def layer_kernel(*refs):
        mine = lax.axis_index("ctx")
        total = refs[ctx][...].astype(F32)
        for rel in range(ctx):
            at = pl.ds(pl.multiple_of((mine ^ rel) * part, part), part)
            total = total + nn_dot(refs[rel][...], refs[ctx + 1][at, :])
        refs[ctx + 2][...] = total.astype(BF)

    layer_args = tuple(gated_own) + (own_rows, out_weight)
    (layer_out,) = call(
        layer_kernel, [shape((own_count, width), BF)], layer_args, 2 * own_count * width * width
    )()(*layer_args)

    def rows_kernel(keep_a, got_a, keep_b, got_b, rows_ref, cot_ref, out_ref):
        for side, (keep, got) in enumerate(((keep_a, got_a), (keep_b, got_b))):
            at = slice(side * half, (side + 1) * half)
            grad = keep[...].astype(F32) + got[...].astype(F32)
            normed, inverse = normalize(rows_ref[at, :].astype(F32))
            mean_grad = jnp.mean(grad, axis=-1, keepdims=True)
            mean_cross = jnp.mean(grad * normed, axis=-1, keepdims=True)
            back = (grad - mean_grad - normed * mean_cross) * inverse
            out_ref[at, :] = (cot_ref[at, :].astype(F32) + back).astype(BF)

    rows_args = tuple(dn_own) + (own_rows, cotangent)
    (row_grads,) = call(
        rows_kernel, [shape((own_count, width), BF)], rows_args, own_count * width * 20
    )()(*rows_args)

    if not packed:
        rev = jnp.array([reverse_bits(each, dps) for each in range(dps)], jnp.int32)
        proj_early, out_early = early_parts
        early_pieces = jnp.concatenate(
            [
                proj_early.reshape(dps, proj_step, part),
                out_early.reshape(dps, out_step, ctx, part)
                .transpose(0, 2, 1, 3)
                .reshape(dps, ctx * out_step, part),
            ],
            axis=1,
        )
        late_pieces = (
            jnp.concatenate(late_parts)
            .reshape(dps, proj_step, 3, part)
            .transpose(0, 2, 1, 3)
            .reshape(dps, late_rows, part)
        )
        early_parts, late_parts = (
            jnp.split(jnp.take(each, rev ^ me_dp, axis=0), 2) for each in (early_pieces, late_pieces)
        )

    def reduce_dp(keep, send):
        for bit in dp_bits:
            total = keep.astype(F32) + swap(send, "dp", bit).astype(F32)
            count = keep.shape[0] // 2
            if count:
                keep, send = total[:count].astype(BF), total[count:].astype(BF)
        return total.astype(BF)

    held = jnp.concatenate([reduce_dp(*early_parts), reduce_dp(*late_parts)], axis=1)
    keys = [0]
    for bit in dp_bits[:1:-1]:
        held = jnp.concatenate([held, swap(held, "dp", bit)])
        keys = keys + [key | bit for key in keys]
    pair = (held, swap(held, "dp", dp_bits[1]))
    arrays, holds = [], []
    for side in range(2):
        for rel, values in spread(pair[side], "ctx", order[side]).items():
            for core, each in enumerate((values, swap(values, "dp", 1))):
                arrays.append(each)
                holds.append([(rel, key | (dp_bits[1] * side) | core) for key in keys])

    if packed:

        def finish_kernel(*refs):
            proj_ref, out_ref = refs[len(arrays) :]
            mine_ctx, mine_dp = lax.axis_index("ctx"), lax.axis_index("dp")
            for ref, pieces in zip(refs, holds):
                for at, (rel_ctx, rel_dp) in enumerate(pieces):
                    column, index = mine_ctx ^ rel_ctx, mine_dp ^ rel_dp
                    rows = pl.ds(pl.multiple_of(index * proj_step, proj_step), proj_step)
                    for each in range(4):
                        first = 0 if each == 0 else early_rows + (each - 1) * proj_step
                        lanes = pl.ds(pl.multiple_of(each * width + column * part, part), part)
                        proj_ref[rows, lanes] = ref[at, first : first + proj_step, :].astype(F32) * grad_scale
                    rows = pl.ds(pl.multiple_of(column * part + index * out_step, out_step), out_step)
                    for each in range(ctx):
                        first = proj_step + each * out_step
                        out_ref[rows, each * part : (each + 1) * part] = (
                            ref[at, first : first + out_step, :].astype(F32) * grad_scale
                        )

        proj_grad, out_grad = call(
            finish_kernel,
            [shape((width, 4 * width), F32), shape((width, width), F32)],
            arrays,
            width * width * 10,
        )()(*arrays)
        return (layer_out, row_grads, proj_grad, out_grad)

    pieces = {key: array[at] for array, hold in zip(arrays, holds) for at, key in enumerate(hold)}
    table = jnp.stack([jnp.stack([pieces[c, d] for d in range(dps)]) for c in range(ctx)])
    table = jnp.take(table, jnp.arange(ctx) ^ me_ctx, axis=0)
    table = jnp.take(table, jnp.arange(dps) ^ me_dp, axis=1).astype(F32) * grad_scale
    split = proj_step + ctx * out_step
    proj_grad = (
        jnp.concatenate([table[:, :, :proj_step], table[:, :, split:]], axis=2)
        .reshape(ctx, dps, 4, proj_step, part)
        .transpose(1, 3, 2, 0, 4)
        .reshape(width, 4 * width)
    )
    out_grad = (
        table[:, :, proj_step:split]
        .reshape(ctx, dps, ctx, out_step, part)
        .transpose(0, 1, 3, 2, 4)
        .reshape(width, width)
    )
    return (layer_out, row_grads, proj_grad, out_grad)


def solution(mesh):
    placed = (
        P(("dp", "ctx"), None),
        P(("dp", "ctx")),
        P(("dp", "ctx")),
        P("dp", None),
        P(),
        P(),
        P(("dp", "ctx"), None),
    )
    return jax.shard_map(
        local,
        mesh=mesh,
        in_specs=placed,
        out_specs=(P(("dp", "ctx"), None), P(("dp", "ctx"), None), P(), P()),
        check_vma=False,
    )
```

```python
import functools

import jax
import jax.numpy as jnp
from jax import lax
from jax.experimental import pallas as pl
from jax.experimental.pallas import tpu as pltpu
from jax.sharding import PartitionSpec as P


HEADS = 8
EPS = 1e-05
TILE = 256
BF = jnp.bfloat16
F32 = jnp.float32
SRC_SHIFT = 16
LOW = 128
EXTRA = 16


def bits_of(count):
    return [1 << each for each in range(count.bit_length() - 1)]


def reverse_bits(value, count):
    width = count.bit_length() - 1
    result = 0
    for each in range(width):
        result = result | (((value >> each) & 1) << (width - 1 - each))
    return result


def swap(values, axis, distance):
    size = lax.axis_size(axis)
    return lax.ppermute(values, axis, [(each, each ^ distance) for each in range(size)])


def spread(values, axis, order):
    held = {0: values}
    for bit in order:
        held.update({key | bit: swap(held[key], axis, bit) for key in sorted(held)})
    return held


def direct(parts, axis):
    return [parts[0]] + [swap(parts[rel], axis, rel) for rel in range(1, len(parts))]


def nt_dot(left, right):
    return lax.dot_general(left, right, (((1,), (1,)), ((), ())), preferred_element_type=F32)


def tn_dot(left, right):
    return lax.dot_general(left, right, (((0,), (0,)), ((), ())), preferred_element_type=F32)


def nn_dot(left, right):
    return jnp.dot(left, right, preferred_element_type=F32)


def normalize(values):
    centre = values - jnp.mean(values, axis=-1, keepdims=True)
    inverse = lax.rsqrt(jnp.mean(centre * centre, axis=-1, keepdims=True) + EPS)
    return centre * inverse, inverse


def silu(values):
    half = 0.5 * values
    return half + half * jnp.tanh(half)


def silu_grad(values):
    half = 0.5 * values
    tanh = jnp.tanh(half)
    return (0.5 + 0.5 * tanh) * (1.0 + half * (1.0 - tanh))


def call(kernel, out_shapes, args, flops, smem=(), hbm=(), limit=16):
    moved = sum(each.size * each.dtype.itemsize for each in list(args) + list(out_shapes))
    specs = [
        pl.BlockSpec(
            memory_space=pltpu.SMEM if index in smem else pltpu.HBM if index in hbm else pltpu.VMEM
        )
        for index in range(len(args))
    ]
    return functools.partial(
        pl.pallas_call,
        kernel,
        out_shape=tuple(out_shapes),
        in_specs=specs,
        out_specs=tuple(pl.BlockSpec(memory_space=pltpu.VMEM) for _ in out_shapes),
        compiler_params=pltpu.CompilerParams(vmem_limit_bytes=limit * 1024 * 1024),
        cost_estimate=pl.CostEstimate(flops=flops, bytes_accessed=moved, transcendentals=0),
    )


def local(loader_rows, send_slot, arrive_slot, user_lengths, proj_weight, out_weight, cotangent):
    own_count = send_slot.shape[0]
    width = out_weight.shape[0]
    users = user_lengths.shape[1]
    ctx = lax.axis_size("ctx")
    dps = lax.axis_size("dp")
    devices = ctx * dps
    per_pair = own_count // devices
    cap = per_pair + max(1, per_pair // 2)
    half = own_count // 2
    rows_all = ctx * own_count
    blocks = 2 * ctx
    part = width // ctx
    heads = HEADS // ctx
    head_dim = width // HEADS
    scale = head_dim ** (-0.5)
    pair_rows = ctx * cap
    side_rows = dps // 2 * pair_rows
    tiles = rows_all // TILE
    ctx_bits = bits_of(ctx)
    me_ctx = lax.axis_index("ctx")
    me_dp = lax.axis_index("dp")
    shape = jax.ShapeDtypeStruct
    dp_bits = bits_of(dps)
    proj_step, out_step = width // dps, part // dps
    piece_rows = 2 * proj_step + ctx // 2 * out_step
    packed = part % 128 == 0 and out_step % 16 == 0
    room = max(20, 20 * rows_all // 1024)
    grad_scale = (own_count * devices) ** (-0.5)

    def block_of(device, side):
        return device if side == 0 else blocks - 1 - device

    def block_rows(device, side):
        return pl.ds(pl.multiple_of(block_of(device, side) * half, half), half)

    def weight_of(ref, column, each):
        if packed:
            return ref[:, pl.ds(pl.multiple_of(each * width + column * part, part), part)]
        return ref[column, :, each * part : (each + 1) * part]

    weights = proj_weight
    if not packed:
        weights = (
            proj_weight.reshape(width, 4, ctx, part).transpose(2, 0, 1, 3).reshape(ctx, width, 4 * part)
        )

    def pack_kernel(slot_hbm, rows_hbm, arrive_hbm, cot_hbm, *refs):
        out_refs, (slot_ref, rows_ref, arrive_ref, sems) = refs[: dps + 1], refs[dps + 1 :]
        mine = lax.axis_index("dp")
        copies = [
            pltpu.make_async_copy(start, end, sems.at[at])
            for at, (start, end) in enumerate(
                (
                    (slot_hbm, slot_ref),
                    (rows_hbm, rows_ref),
                    (arrive_hbm, arrive_ref),
                    (cot_hbm, out_refs[dps].at[pl.ds(0, own_count), :]),
                )
            )
        ]
        for each in copies:
            each.start()
        for each in copies:
            each.wait()
        slot = slot_ref[...]
        rows = rows_ref[...]
        row_id = lax.broadcasted_iota(jnp.int32, (pair_rows, own_count), 0)
        for rel in range(dps):
            picked = (row_id + (mine ^ rel) * pair_rows == slot).astype(BF)
            out_refs[rel][...] = nn_dot(picked, rows).astype(BF)
        cot_ref = out_refs[dps]
        arrive = arrive_ref[...]
        source = jnp.floor((arrive.astype(F32) + 0.5) * (1.0 / cap)).astype(jnp.int32)
        place = arrive - source * cap
        base = ((source >> len(ctx_bits)) ^ mine) * pair_rows + lax.axis_index("ctx") * cap + place
        line = lax.broadcasted_iota(jnp.int32, (EXTRA, own_count), 0)
        table = jnp.where(
            line == 0, source & (ctx - 1), jnp.where(line == 1, base // LOW, base % LOW)
        )
        cot_ref[own_count:, :] = jnp.zeros((EXTRA, width), BF)
        cot_ref[own_count:, :own_count] = table.astype(F32).astype(BF)

    pack_args = (
        send_slot.reshape(1, own_count),
        loader_rows,
        arrive_slot.reshape(1, own_count),
        cotangent,
    )
    pack_outs = [shape((pair_rows, width), BF)] * dps + [shape((own_count + EXTRA, width), BF)]
    *sent, cot_own = call(
        pack_kernel, pack_outs, pack_args, 2 * dps * pair_rows * own_count * width, hbm=range(4), limit=60
    )(
        scratch_shapes=[
            pltpu.VMEM((1, own_count), jnp.int32),
            pltpu.VMEM((own_count, width), BF),
            pltpu.VMEM((1, own_count), jnp.int32),
            pltpu.SemaphoreType.DMA((4,)),
        ]
    )(*pack_args)
    cot_of = direct([cot_own] * ctx, "ctx")
    landed = direct(sent, "dp")
    sides = (
        spread(jnp.concatenate(landed[: dps // 2]), "ctx", ctx_bits),
        spread(jnp.concatenate(landed[dps // 2 :]), "ctx", ctx_bits[::-1]),
    )

    def prepare_kernel(lengths_ref, weight_ref, out_weight_ref, own_ref, out_own_ref, begin_ref):
        mine = lax.axis_index("ctx")
        for each in range(4):
            own_ref[:, each * part : (each + 1) * part] = weight_of(weight_ref, mine, each)
        out_own_ref[...] = out_weight_ref[pl.ds(pl.multiple_of(mine * part, part), part), :]
        position = lax.broadcasted_iota(jnp.int32, (blocks, half), 0) * half + lax.broadcasted_iota(
            jnp.int32, (blocks, half), 1
        )
        end = 0
        begin = jnp.zeros((blocks, half), jnp.int32)
        for each in range(users):
            length = lengths_ref[0, each]
            end = end + length
            begin = begin + jnp.where(position >= end, length, 0)
        begin_ref[...] = begin

    prepare_args = (user_lengths, weights, out_weight)
    prepare_outs = [shape((width, 4 * part), BF), shape((part, width), BF), shape((blocks, half), jnp.int32)]
    proj_own, out_own, begin_of = call(prepare_kernel, prepare_outs, prepare_args, width * width, smem=(0,))()(
        *prepare_args
    )

    def lane_masks():
        lane = lax.broadcasted_iota(jnp.int32, (1, part), 1)
        return [
            (lane >= each * head_dim) & (lane < (each + 1) * head_dim) for each in range(heads)
        ]

    def forward_kernel(*refs):
        side_refs = (refs[:ctx], refs[ctx : 2 * ctx])
        cot_refs = refs[2 * ctx : 3 * ctx]
        begin_ref, own_weight_ref, out_own_ref = refs[3 * ctx : 3 * ctx + 3]
        own_ref, norm_t_ref, pre_ref, proj_ref, att_ref, gg_ref, stat_ref = refs[3 * ctx + 3 : 3 * ctx + 10]
        where_ref, rows_ref, query_ref, value_ref = refs[3 * ctx + 10 :]
        mine = lax.axis_index("ctx")
        out_own = out_own_ref[...]
        begins = jnp.transpose(begin_ref[...].astype(F32)).astype(jnp.int32)
        for rel in range(ctx):
            table = jnp.transpose(cot_refs[rel][own_count:, :own_count].astype(F32)[:8, :])
            column = (table[:, 0:1].astype(jnp.int32) << SRC_SHIFT) + (
                table[:, 1:2] * LOW + table[:, 2:3]
            ).astype(jnp.int32)
            for side in range(2):
                here = slice(side * half, (side + 1) * half)
                where_ref[block_rows(mine ^ rel, side), :] = column[here, :]
                gg_ref[block_rows(mine ^ rel, side), :] = nt_dot(cot_refs[rel][here, :], out_own)
        masks = lane_masks()
        source_row = lax.broadcasted_iota(jnp.int32, (TILE, side_rows), 1)
        for tile in range(tiles):
            span = pl.ds(tile * TILE, TILE)
            wanted = where_ref[span, :]
            total = jnp.zeros((TILE, width), F32)
            for rel in range(ctx):
                for side in range(2):
                    key = source_row + (((mine ^ rel) << SRC_SHIFT) + side * side_rows)
                    picked = (key == wanted).astype(BF)
                    total = total + nn_dot(picked, side_refs[side][rel][...])
            rows_ref[span, :] = total.astype(BF)
            normed = normalize(total)[0].astype(BF)
            norm_t_ref[:, tile * TILE : (tile + 1) * TILE] = jnp.transpose(normed)
            pre = nn_dot(normed, own_weight_ref[...])
            pre_ref[span, :] = pre
            proj = silu(pre).astype(BF)
            proj_ref[span, :] = proj
            query = proj[:, 2 * part : 3 * part] * jnp.asarray(0.5 * scale, BF)
            value = proj[:, part : 2 * part]
            for head in range(heads):
                query_ref[head, span, :] = jnp.where(masks[head], query, jnp.zeros_like(query))
                value_ref[head, span, :] = jnp.where(masks[head], value, jnp.zeros_like(value))
        for side in range(2):
            own_ref[side * half : (side + 1) * half, :] = rows_ref[block_rows(mine, side), :]
        for at in range(tiles):
            span = pl.ds(at * TILE, TILE)
            query_pos = lax.broadcasted_iota(jnp.int32, (TILE, 1), 0) + at * TILE
            begin = jnp.concatenate(
                [begins[:, each : each + 1] for each in range(at * TILE // half, (at + 1) * TILE // half)]
            )
            total = jnp.zeros((TILE, part), F32)
            for key_at in range(at + 1):
                key_span = pl.ds(key_at * TILE, TILE)
                key_pos = lax.broadcasted_iota(jnp.int32, (1, TILE), 1) + key_at * TILE
                allowed = key_pos >= begin
                if key_at == at:
                    allowed = allowed & (key_pos <= query_pos)
                key = proj_ref[key_span, 3 * part :]
                for head in range(heads):
                    score = nt_dot(query_ref[head, span, :], key)
                    weight = jnp.where(allowed, score + score * jnp.tanh(score), 0.0).astype(BF)
                    total = total + nn_dot(weight, value_ref[head, key_span, :])
            att_ref[span, :] = total
            grad = gg_ref[span, :] * proj_ref[span, :part].astype(F32)
            mean = jnp.mean(total, axis=-1, keepdims=True)
            centre = total - mean
            spread_sum = jnp.sum(centre * centre, axis=-1, keepdims=True)
            grad_sum = jnp.sum(grad, axis=-1, keepdims=True)
            cross_sum = jnp.sum(grad * centre, axis=-1, keepdims=True)
            lane = lax.broadcasted_iota(jnp.int32, (TILE, 128), 1)
            table = jnp.where(
                lane == 0, mean, jnp.where(lane == 1, spread_sum, jnp.where(lane == 2, grad_sum, cross_sum))
            )
            for sub in range(TILE // half):
                turned = jnp.transpose(table[sub * half : (sub + 1) * half, :])
                block = at * (TILE // half) + sub
                for each in range(4):
                    stat_ref[each, block : block + 1, :] = turned[each : each + 1, :]

    fwd_args = (
        tuple(sides[0][rel] for rel in range(ctx))
        + tuple(sides[1][rel] for rel in range(ctx))
        + tuple(cot_of)
        + (begin_of, proj_own, out_own)
    )
    fwd_outs = [
        shape((own_count, width), BF),
        shape((width, rows_all), BF),
        shape((rows_all, 4 * part), F32),
        shape((rows_all, 4 * part), BF),
        shape((rows_all, part), F32),
        shape((rows_all, part), F32),
        shape((4, blocks, half), F32),
    ]
    own_rows, norm_t, pre, proj, attended, grad_gated, stats = call(
        forward_kernel, fwd_outs, fwd_args, 4 * rows_all * rows_all * part, limit=room
    )(
        scratch_shapes=[
            pltpu.VMEM((rows_all, 1), jnp.int32),
            pltpu.VMEM((rows_all, width), BF),
            pltpu.VMEM((heads, rows_all, part), BF),
            pltpu.VMEM((heads, rows_all, part), BF),
        ]
    )(*fwd_args)

    stats_of = direct([stats] * ctx, "ctx")

    grad_count = 4 if packed else 2

    def proj_places(chunk):
        return [(at * proj_step, 2 * chunk + at) for at in range(2)]

    def out_places(chunk):
        return [(2 * proj_step + at * out_step, ctx // 2 * chunk + at) for at in range(ctx // 2)]

    def backward_kernel(*refs):
        stat_refs, cot_refs = refs[:ctx], refs[ctx : 2 * ctx]
        begin_ref, att_ref, gg_ref, pre_ref, proj_ref, norm_t_ref = refs[2 * ctx : 2 * ctx + 6]
        grad_refs, refs = refs[2 * ctx + 6 : 2 * ctx + 6 + grad_count], refs[2 * ctx + 6 + grad_count :]
        row_refs = refs[:ctx]
        query_ref, key_ref, grad_ref, dq_ref, gp_ref, gated_ref, late_ref, out_ref = refs[ctx:]
        mine = lax.axis_index("ctx")
        masks = lane_masks()

        def masked(values, head):
            return jnp.where(masks[head], values, jnp.zeros_like(values))

        means = [each[0] for each in stat_refs]
        mean = sum(means) / ctx
        spread_sum = sum(each[1] + part * (own - mean) ** 2 for each, own in zip(stat_refs, means))
        inverse = lax.rsqrt(spread_sum / width + EPS)
        grad_mean = sum(each[2] for each in stat_refs) / width
        cross = sum(each[3] + each[2] * (own - mean) for each, own in zip(stat_refs, means))
        cross_mean = inverse * cross / width
        for block in range(blocks):
            span = pl.ds(block * half, half)
            table = jnp.concatenate(
                [each[block : block + 1, :] for each in (mean, inverse, grad_mean, cross_mean)] * 2
            )
            columns = jnp.transpose(table)
            mean_c, inverse_c, grad_c, cross_c = (columns[:, each : each + 1] for each in range(4))
            normed = (att_ref[span, :] - mean_c) * inverse_c
            grad = gg_ref[span, :]
            update = proj_ref[span, :part].astype(F32)
            gated_ref[span, :] = (normed * update).astype(BF)
            grad_att = ((grad * update - grad_c - normed * cross_c) * inverse_c).astype(BF)
            gp_ref[span, :part] = (grad * normed * silu_grad(pre_ref[span, :part])).astype(BF)
            query = proj_ref[span, 2 * part : 3 * part] * jnp.asarray(0.5 * scale, BF)
            for head in range(heads):
                query_ref[head, span, :] = masked(query, head)
                key_ref[head, span, :] = masked(proj_ref[span, 3 * part :], head)
                grad_ref[head, span, :] = masked(grad_att, head)
            dq_ref[span, :] = jnp.zeros((half, part), F32)
        out_term = jnp.zeros((part, width), F32)
        for rel in range(ctx):
            for side in range(2):
                here = slice(side * half, (side + 1) * half)
                gated = gated_ref[block_rows(mine ^ rel, side), :]
                row_refs[rel][here, 4 * part :] = gated
            out_term = out_term + tn_dot(row_refs[rel][:, 4 * part :], cot_refs[rel][:own_count, :])
        out_ref[...] = out_term.astype(BF)
        for key_at in range(tiles):
            key_span = pl.ds(key_at * TILE, TILE)
            key_pos = lax.broadcasted_iota(jnp.int32, (TILE, 1), 0) + key_at * TILE
            key = proj_ref[key_span, 3 * part :]
            value = proj_ref[key_span, part : 2 * part] * jnp.asarray(0.5 * scale, BF)
            grad_key = jnp.zeros((TILE, part), F32)
            grad_value = jnp.zeros((TILE, part), F32)
            for at in range(key_at, tiles):
                span = pl.ds(at * TILE, TILE)
                query_pos = lax.broadcasted_iota(jnp.int32, (1, TILE), 1) + at * TILE
                begin = jnp.concatenate(
                    [
                        begin_ref[each : each + 1, :]
                        for each in range(at * TILE // half, (at + 1) * TILE // half)
                    ],
                    axis=1,
                )
                allowed = key_pos >= begin
                if at == key_at:
                    allowed = allowed & (key_pos <= query_pos)
                grad_query = jnp.zeros((TILE, part), F32)
                for head in range(heads):
                    score = nt_dot(key, query_ref[head, span, :])
                    tanh = jnp.tanh(score)
                    cross = score * tanh
                    weight = jnp.where(allowed, score + cross, 0.0).astype(BF)
                    grad_value = grad_value + nn_dot(weight, grad_ref[head, span, :])
                    grad_weight = nt_dot(value, grad_ref[head, span, :])
                    slope = (1.0 + tanh) * (1.0 + score - cross)
                    grad_score = jnp.where(allowed, grad_weight * slope, 0.0).astype(BF)
                    grad_key = grad_key + nn_dot(grad_score, query_ref[head, span, :])
                    grad_query = grad_query + tn_dot(grad_score, key_ref[head, key_span, :])
                dq_ref[span, :] = dq_ref[span, :] + grad_query
            gp_ref[key_span, part : 2 * part] = (
                grad_value * silu_grad(pre_ref[key_span, part : 2 * part])
            ).astype(BF)
            gp_ref[key_span, 3 * part :] = (
                grad_key * (2.0 / scale) * silu_grad(pre_ref[key_span, 3 * part :])
            ).astype(BF)
        for tile in range(tiles):
            span = pl.ds(tile * TILE, TILE)
            gp_ref[span, 2 * part : 3 * part] = (
                dq_ref[span, :] * silu_grad(pre_ref[span, 2 * part : 3 * part])
            ).astype(BF)
        for rel in range(ctx):
            for side in range(2):
                row_refs[rel][side * half : (side + 1) * half, : 4 * part] = gp_ref[
                    block_rows(mine ^ rel, side), :
                ]
        late_ref[...] = nn_dot(norm_t_ref[...], gp_ref[...]).astype(BF)
        if not packed:
            grad_refs[0][...] = late_ref[...]
            grad_refs[1][...] = out_ref[...]
            return
        mine = lax.axis_index("dp")
        for slot in range(dps):
            index = reverse_bits(slot, dps) ^ mine
            rows = pl.ds(pl.multiple_of(index * proj_step, proj_step), proj_step)
            out_rows = pl.ds(pl.multiple_of(index * out_step, out_step), out_step)
            for chunk in range(2):
                to = grad_refs[2 * chunk + slot // (dps // 2)].at[slot % (dps // 2)]
                for first, each in proj_places(chunk):
                    to[first : first + proj_step, :] = late_ref[rows, each * part : (each + 1) * part]
                for first, each in out_places(chunk):
                    to[first : first + out_step, :] = out_ref[out_rows, each * part : (each + 1) * part]

    bwd_args = (*stats_of, *cot_of, begin_of, attended, grad_gated, pre, proj, norm_t)
    if packed:
        bwd_outs = [shape((dps // 2, piece_rows, part), BF)] * 4
    else:
        bwd_outs = [shape((width, 4 * part), BF), shape((part, width), BF)]
    bwd_outs = bwd_outs + [shape((own_count, 5 * part), BF)] * ctx
    results = call(
        backward_kernel, bwd_outs, bwd_args, 10 * rows_all * rows_all * part, limit=room
    )(
        scratch_shapes=[
            pltpu.VMEM((heads, rows_all, part), BF),
            pltpu.VMEM((heads, rows_all, part), BF),
            pltpu.VMEM((heads, rows_all, part), BF),
            pltpu.VMEM((rows_all, part), F32),
            pltpu.VMEM((rows_all, 4 * part), BF),
            pltpu.VMEM((rows_all, part), BF),
            pltpu.VMEM((width, 4 * part), BF),
            pltpu.VMEM((part, width), BF),
        ]
    )(*bwd_args)

    grad_parts, row_parts = results[:grad_count], results[grad_count:]

    if not packed:
        rev = jnp.array([reverse_bits(each, dps) for each in range(dps)], jnp.int32)
        proj_blocks = grad_parts[0].reshape(dps, proj_step, 4, part).transpose(0, 2, 1, 3)
        out_blocks = grad_parts[1].reshape(dps, out_step, ctx, part).transpose(0, 2, 1, 3)
        grad_parts = []
        for chunk in range(2):
            pieces = jnp.concatenate(
                [
                    proj_blocks[:, 2 * chunk : 2 * chunk + 2].reshape(dps, -1, part),
                    out_blocks[:, ctx // 2 * chunk : ctx // 2 * (chunk + 1)].reshape(dps, -1, part),
                ],
                axis=1,
            )
            grad_parts += jnp.split(jnp.take(pieces, rev ^ me_dp, axis=0), 2)

    def add_kernel(keep_ref, got_ref, *out_refs):
        count = out_refs[0].shape[0]
        for at, ref in enumerate(out_refs):
            here = slice(at * count, (at + 1) * count)
            ref[...] = (keep_ref[here].astype(F32) + got_ref[here].astype(F32)).astype(BF)

    def exchange_kernel(keep_ref, got_ref, out_ref):
        for at in range(2):
            total = keep_ref[at].astype(F32) + got_ref[1 - at].astype(F32)
            out_ref[at] = total.astype(BF)

    def reduce_dp(keep, send):
        for bit in dp_bits[:-1]:
            got = swap(send, "dp", bit)
            count = keep.shape[0] // 2
            last = count == 1
            outs = [shape((2 if last else count, piece_rows, part), BF)] * (1 if last else 2)
            keep, *send = call(add_kernel, outs, (keep, got), keep.size)()(keep, got)
            send = send[0] if send else None
        got = swap(keep, "dp", dp_bits[-1])
        return call(exchange_kernel, [shape(keep.shape, BF)], (keep, got), keep.size)()(keep, got)[0]

    held = [reduce_dp(*grad_parts[2 * chunk : 2 * chunk + 2]) for chunk in range(2)]
    keys = [0, dp_bits[-1]]
    row_own = direct(row_parts, "ctx")

    def rows_kernel(*refs):
        part_refs, (rows_ref, cot_ref, weight_ref, out_weight_ref, layer_ref, grad_ref) = refs[:ctx], refs[ctx:]
        mine = lax.axis_index("ctx")
        rows = rows_ref[...].astype(F32)
        layer = rows
        grad = jnp.zeros((own_count, width), F32)
        for rel in range(ctx):
            column = mine ^ rel
            at = pl.ds(pl.multiple_of(column * part, part), part)
            layer = layer + nn_dot(part_refs[rel][:, 4 * part :], out_weight_ref[at, :])
            for each in range(4):
                grad = grad + nt_dot(
                    part_refs[rel][:, each * part : (each + 1) * part], weight_of(weight_ref, column, each)
                )
        layer_ref[...] = layer.astype(BF)
        normed, inverse = normalize(rows)
        mean_grad = jnp.mean(grad, axis=-1, keepdims=True)
        mean_cross = jnp.mean(grad * normed, axis=-1, keepdims=True)
        back = (grad - mean_grad - normed * mean_cross) * inverse
        grad_ref[...] = (cot_ref[...].astype(F32) + back).astype(BF)

    rows_args = tuple(row_own) + (own_rows, cotangent, weights, out_weight)
    layer_out, row_grads = call(
        rows_kernel, [shape((own_count, width), BF)] * 2, rows_args, 10 * own_count * width * width
    )()(*rows_args)

    for bit in dp_bits[-2:0:-1]:
        held = [jnp.concatenate([each, swap(each, "dp", bit)]) for each in held]
        keys = keys + [key | bit for key in keys]
    order = (ctx_bits, ctx_bits[::-1])
    arrays, holds = [], []
    groups = [[], [], []]
    for chunk in range(2):
        for rel, values in spread(held[chunk], "ctx", order[chunk]).items():
            arrays.append(values)
            holds.append([(chunk, rel, key) for key in keys])
            groups[0 if rel == 0 else 2 if rel == ctx - 1 else 1].append(len(holds) - 1)
    for group in groups:
        both = jnp.concatenate([arrays[each] for each in group])
        arrays.append(swap(both, "dp", 1))
        holds.append([(chunk, rel, key | 1) for each in group for chunk, rel, key in holds[each]])

    if packed:

        def finish_kernel(*refs):
            proj_ref, out_ref = refs[len(arrays) :]
            mine_ctx, mine_dp = lax.axis_index("ctx"), lax.axis_index("dp")
            for ref, pieces in zip(refs, holds):
                for at, (chunk, rel_ctx, rel_dp) in enumerate(pieces):
                    column, index = mine_ctx ^ rel_ctx, mine_dp ^ rel_dp
                    rows = pl.ds(pl.multiple_of(index * proj_step, proj_step), proj_step)
                    for first, each in proj_places(chunk):
                        lanes = pl.ds(pl.multiple_of(each * width + column * part, part), part)
                        proj_ref[rows, lanes] = ref[at, first : first + proj_step, :].astype(F32) * grad_scale
                    rows = pl.ds(pl.multiple_of(column * part + index * out_step, out_step), out_step)
                    for first, each in out_places(chunk):
                        out_ref[rows, each * part : (each + 1) * part] = (
                            ref[at, first : first + out_step, :].astype(F32) * grad_scale
                        )

        proj_grad, out_grad = call(
            finish_kernel,
            [shape((width, 4 * width), F32), shape((width, width), F32)],
            arrays,
            width * width * 10,
        )()(*arrays)
        return (layer_out, row_grads, proj_grad, out_grad)

    pieces = {key: array[at] for array, hold in zip(arrays, holds) for at, key in enumerate(hold)}
    table = jnp.stack(
        [
            jnp.stack([jnp.stack([pieces[chunk, c, d] for chunk in range(2)]) for d in range(dps)])
            for c in range(ctx)
        ]
    )
    table = jnp.take(table, jnp.arange(ctx) ^ me_ctx, axis=0)
    table = jnp.take(table, jnp.arange(dps) ^ me_dp, axis=1).astype(F32) * grad_scale
    proj_grad = (
        table[:, :, :, : 2 * proj_step]
        .reshape(ctx, dps, 4, proj_step, part)
        .transpose(1, 3, 2, 0, 4)
        .reshape(width, 4 * width)
    )
    out_grad = (
        table[:, :, :, 2 * proj_step :]
        .reshape(ctx, dps, ctx, out_step, part)
        .transpose(0, 1, 3, 2, 4)
        .reshape(width, width)
    )
    return (layer_out, row_grads, proj_grad, out_grad)


def solution(mesh):
    placed = (
        P(("dp", "ctx"), None),
        P(("dp", "ctx")),
        P(("dp", "ctx")),
        P("dp", None),
        P(),
        P(),
        P(("dp", "ctx"), None),
    )

    return jax.shard_map(
        local,
        mesh=mesh,
        in_specs=placed,
        out_specs=(P(("dp", "ctx"), None), P(("dp", "ctx"), None), P(), P()),
        check_vma=False,
    )
```

```python
import functools

import jax
import jax.numpy as jnp
from jax import lax
from jax.experimental import pallas as pl
from jax.experimental.pallas import tpu as pltpu
from jax.sharding import PartitionSpec as P


HEADS = 8
EPS = 1e-05
TILE = 256
BF = jnp.bfloat16
F32 = jnp.float32
SRC_SHIFT = 16
LOW = 128
EXTRA = 16


def bits_of(count):
    return [1 << each for each in range(count.bit_length() - 1)]


def reverse_bits(value, count):
    width = count.bit_length() - 1
    result = 0
    for each in range(width):
        result = result | (((value >> each) & 1) << (width - 1 - each))
    return result


def swap(values, axis, distance):
    size = lax.axis_size(axis)
    return lax.ppermute(values, axis, [(each, each ^ distance) for each in range(size)])


def spread(values, axis, order):
    held = {0: values}
    for bit in order:
        held.update({key | bit: swap(held[key], axis, bit) for key in sorted(held)})
    return held


def direct(parts, axis):
    return [parts[0]] + [swap(parts[rel], axis, rel) for rel in range(1, len(parts))]


def nt_dot(left, right):
    return lax.dot_general(left, right, (((1,), (1,)), ((), ())), preferred_element_type=F32)


def tn_dot(left, right):
    return lax.dot_general(left, right, (((0,), (0,)), ((), ())), preferred_element_type=F32)


def nn_dot(left, right):
    return jnp.dot(left, right, preferred_element_type=F32)


def normalize(values):
    centre = values - jnp.mean(values, axis=-1, keepdims=True)
    inverse = lax.rsqrt(jnp.mean(centre * centre, axis=-1, keepdims=True) + EPS)
    return centre * inverse, inverse


def silu(values):
    half = 0.5 * values
    return half + half * jnp.tanh(half)


def silu_grad(values):
    half = 0.5 * values
    tanh = jnp.tanh(half)
    return (0.5 + 0.5 * tanh) * (1.0 + half * (1.0 - tanh))


def call(kernel, out_shapes, args, flops, smem=(), hbm=(), limit=16):
    moved = sum(each.size * each.dtype.itemsize for each in list(args) + list(out_shapes))
    specs = [
        pl.BlockSpec(
            memory_space=pltpu.SMEM if index in smem else pltpu.HBM if index in hbm else pltpu.VMEM
        )
        for index in range(len(args))
    ]
    return functools.partial(
        pl.pallas_call,
        kernel,
        out_shape=tuple(out_shapes),
        in_specs=specs,
        out_specs=tuple(pl.BlockSpec(memory_space=pltpu.VMEM) for _ in out_shapes),
        compiler_params=pltpu.CompilerParams(vmem_limit_bytes=limit * 1024 * 1024),
        cost_estimate=pl.CostEstimate(flops=flops, bytes_accessed=moved, transcendentals=0),
    )


def local(loader_rows, send_slot, arrive_slot, user_lengths, proj_weight, out_weight, cotangent):
    own_count = send_slot.shape[0]
    width = out_weight.shape[0]
    users = user_lengths.shape[1]
    ctx = lax.axis_size("ctx")
    dps = lax.axis_size("dp")
    devices = ctx * dps
    per_pair = own_count // devices
    cap = per_pair + max(1, per_pair // 2)
    half = own_count // 2
    rows_all = ctx * own_count
    blocks = 2 * ctx
    part = width // ctx
    heads = HEADS // ctx
    head_dim = width // HEADS
    scale = head_dim ** (-0.5)
    pair_rows = ctx * cap
    side_rows = dps // 2 * pair_rows
    tiles = rows_all // TILE
    ctx_bits = bits_of(ctx)
    me_ctx = lax.axis_index("ctx")
    me_dp = lax.axis_index("dp")
    shape = jax.ShapeDtypeStruct
    dp_bits = bits_of(dps)
    proj_step, out_step = width // dps, part // dps
    piece_rows = 2 * proj_step + ctx // 2 * out_step
    packed = part % 128 == 0 and out_step % 16 == 0
    room = max(20, 20 * rows_all // 1024)
    grad_scale = (own_count * devices) ** (-0.5)

    def block_of(device, side):
        return device if side == 0 else blocks - 1 - device

    def block_rows(device, side):
        return pl.ds(pl.multiple_of(block_of(device, side) * half, half), half)

    def weight_of(ref, column, each):
        if packed:
            return ref[:, pl.ds(pl.multiple_of(each * width + column * part, part), part)]
        return ref[column, :, each * part : (each + 1) * part]

    weights = proj_weight
    if not packed:
        weights = (
            proj_weight.reshape(width, 4, ctx, part).transpose(2, 0, 1, 3).reshape(ctx, width, 4 * part)
        )

    def pack_kernel(slot_hbm, rows_hbm, arrive_hbm, cot_hbm, *refs):
        out_refs, (slot_ref, rows_ref, arrive_ref, sems) = refs[: dps + 1], refs[dps + 1 :]
        mine = lax.axis_index("dp")
        copies = [
            pltpu.make_async_copy(start, end, sems.at[at])
            for at, (start, end) in enumerate(
                (
                    (slot_hbm, slot_ref),
                    (rows_hbm, rows_ref),
                    (arrive_hbm, arrive_ref),
                    (cot_hbm, out_refs[dps].at[pl.ds(0, own_count), :]),
                )
            )
        ]
        for each in copies:
            each.start()
        for each in copies:
            each.wait()
        slot = slot_ref[...]
        rows = rows_ref[...]
        row_id = lax.broadcasted_iota(jnp.int32, (pair_rows, own_count), 0)
        for rel in range(dps):
            picked = (row_id + (mine ^ rel) * pair_rows == slot).astype(BF)
            out_refs[rel][...] = nn_dot(picked, rows).astype(BF)
        cot_ref = out_refs[dps]
        arrive = arrive_ref[...]
        source = jnp.floor((arrive.astype(F32) + 0.5) * (1.0 / cap)).astype(jnp.int32)
        place = arrive - source * cap
        base = ((source >> len(ctx_bits)) ^ mine) * pair_rows + lax.axis_index("ctx") * cap + place
        line = lax.broadcasted_iota(jnp.int32, (EXTRA, own_count), 0)
        table = jnp.where(
            line == 0, source & (ctx - 1), jnp.where(line == 1, base // LOW, base % LOW)
        )
        cot_ref[own_count:, :] = jnp.zeros((EXTRA, width), BF)
        cot_ref[own_count:, :own_count] = table.astype(F32).astype(BF)

    pack_args = (
        send_slot.reshape(1, own_count),
        loader_rows,
        arrive_slot.reshape(1, own_count),
        cotangent,
    )
    pack_outs = [shape((pair_rows, width), BF)] * dps + [shape((own_count + EXTRA, width), BF)]
    *sent, cot_own = call(
        pack_kernel, pack_outs, pack_args, 2 * dps * pair_rows * own_count * width, hbm=range(4), limit=60
    )(
        scratch_shapes=[
            pltpu.VMEM((1, own_count), jnp.int32),
            pltpu.VMEM((own_count, width), BF),
            pltpu.VMEM((1, own_count), jnp.int32),
            pltpu.SemaphoreType.DMA((4,)),
        ]
    )(*pack_args)
    cot_of = direct([cot_own] * ctx, "ctx")
    landed = direct(sent, "dp")
    sides = (
        spread(jnp.concatenate(landed[: dps // 2]), "ctx", ctx_bits),
        spread(jnp.concatenate(landed[dps // 2 :]), "ctx", ctx_bits[::-1]),
    )

    def prepare_kernel(lengths_ref, weight_ref, out_weight_ref, own_ref, out_own_ref, begin_ref):
        mine = lax.axis_index("ctx")
        for each in range(4):
            own_ref[:, each * part : (each + 1) * part] = weight_of(weight_ref, mine, each)
        out_own_ref[...] = out_weight_ref[pl.ds(pl.multiple_of(mine * part, part), part), :]
        position = lax.broadcasted_iota(jnp.int32, (blocks, half), 0) * half + lax.broadcasted_iota(
            jnp.int32, (blocks, half), 1
        )
        end = 0
        begin = jnp.zeros((blocks, half), jnp.int32)
        for each in range(users):
            length = lengths_ref[0, each]
            end = end + length
            begin = begin + jnp.where(position >= end, length, 0)
        begin_ref[...] = begin

    prepare_args = (user_lengths, weights, out_weight)
    prepare_outs = [shape((width, 4 * part), BF), shape((part, width), BF), shape((blocks, half), jnp.int32)]
    proj_own, out_own, begin_of = call(prepare_kernel, prepare_outs, prepare_args, width * width, smem=(0,))()(
        *prepare_args
    )

    def lane_masks():
        lane = lax.broadcasted_iota(jnp.int32, (1, part), 1)
        return [
            (lane >= each * head_dim) & (lane < (each + 1) * head_dim) for each in range(heads)
        ]

    def forward_kernel(*refs):
        side_refs = (refs[:ctx], refs[ctx : 2 * ctx])
        cot_refs = refs[2 * ctx : 3 * ctx]
        begin_ref, own_weight_ref, out_own_ref = refs[3 * ctx : 3 * ctx + 3]
        own_ref, normed_ref, pre_ref, proj_ref, att_ref, gg_ref, stat_ref = refs[3 * ctx + 3 : 3 * ctx + 10]
        where_ref, rows_ref, query_ref, value_ref, key_t_ref = refs[3 * ctx + 10 :]
        mine = lax.axis_index("ctx")
        out_own = out_own_ref[...]
        begins = jnp.transpose(begin_ref[...].astype(F32)).astype(jnp.int32)
        for rel in range(ctx):
            table = jnp.transpose(cot_refs[rel][own_count:, :own_count].astype(F32)[:8, :])
            column = (table[:, 0:1].astype(jnp.int32) << SRC_SHIFT) + (
                table[:, 1:2] * LOW + table[:, 2:3]
            ).astype(jnp.int32)
            for side in range(2):
                here = slice(side * half, (side + 1) * half)
                where_ref[block_rows(mine ^ rel, side), :] = column[here, :]
                gg_ref[block_rows(mine ^ rel, side), :] = nt_dot(cot_refs[rel][here, :], out_own)
        masks = lane_masks()
        source_row = lax.broadcasted_iota(jnp.int32, (TILE, side_rows), 1)
        for tile in range(tiles):
            span = pl.ds(tile * TILE, TILE)
            wanted = where_ref[span, :]
            total = jnp.zeros((TILE, width), F32)
            for rel in range(ctx):
                for side in range(2):
                    key = source_row + (((mine ^ rel) << SRC_SHIFT) + side * side_rows)
                    picked = (key == wanted).astype(BF)
                    total = total + nn_dot(picked, side_refs[side][rel][...])
            rows_ref[span, :] = total.astype(BF)
            normed = normalize(total)[0].astype(BF)
            normed_ref[span, :] = normed
            pre = nn_dot(normed, own_weight_ref[...])
            pre_ref[span, :] = pre
            proj = silu(pre).astype(BF)
            proj_ref[span, :] = proj
            query = proj[:, 2 * part : 3 * part] * jnp.asarray(0.5 * scale, BF)
            value = proj[:, part : 2 * part]
            key_t_ref[:, tile * TILE : (tile + 1) * TILE] = jnp.transpose(proj[:, 3 * part :])
            for head in range(heads):
                query_ref[head, span, :] = jnp.where(masks[head], query, jnp.zeros_like(query))
                value_ref[head, span, :] = jnp.where(masks[head], value, jnp.zeros_like(value))
        for side in range(2):
            own_ref[side * half : (side + 1) * half, :] = rows_ref[block_rows(mine, side), :]
        for at in range(tiles):
            span = pl.ds(at * TILE, TILE)
            query_pos = lax.broadcasted_iota(jnp.int32, (TILE, 1), 0) + at * TILE
            begin = jnp.concatenate(
                [begins[:, each : each + 1] for each in range(at * TILE // half, (at + 1) * TILE // half)]
            )
            total = jnp.zeros((TILE, part), F32)
            for key_at in range(at + 1):
                key_span = pl.ds(key_at * TILE, TILE)
                key_pos = lax.broadcasted_iota(jnp.int32, (1, TILE), 1) + key_at * TILE
                allowed = key_pos >= begin
                if key_at == at:
                    allowed = allowed & (key_pos <= query_pos)
                key = key_t_ref[:, key_at * TILE : (key_at + 1) * TILE]
                for head in range(heads):
                    score = nn_dot(query_ref[head, span, :], key)
                    weight = jnp.where(allowed, score + score * jnp.tanh(score), 0.0).astype(BF)
                    total = total + nn_dot(weight, value_ref[head, key_span, :])
            att_ref[span, :] = total
            grad = gg_ref[span, :] * proj_ref[span, :part].astype(F32)
            mean = jnp.mean(total, axis=-1, keepdims=True)
            centre = total - mean
            spread_sum = jnp.sum(centre * centre, axis=-1, keepdims=True)
            grad_sum = jnp.sum(grad, axis=-1, keepdims=True)
            cross_sum = jnp.sum(grad * centre, axis=-1, keepdims=True)
            lane = lax.broadcasted_iota(jnp.int32, (TILE, 128), 1)
            table = jnp.where(
                lane == 0, mean, jnp.where(lane == 1, spread_sum, jnp.where(lane == 2, grad_sum, cross_sum))
            )
            for sub in range(TILE // half):
                turned = jnp.transpose(table[sub * half : (sub + 1) * half, :])
                block = at * (TILE // half) + sub
                for each in range(4):
                    stat_ref[each, block : block + 1, :] = turned[each : each + 1, :]

    fwd_args = (
        tuple(sides[0][rel] for rel in range(ctx))
        + tuple(sides[1][rel] for rel in range(ctx))
        + tuple(cot_of)
        + (begin_of, proj_own, out_own)
    )
    fwd_outs = [
        shape((own_count, width), BF),
        shape((rows_all, width), BF),
        shape((rows_all, 4 * part), F32),
        shape((rows_all, 4 * part), BF),
        shape((rows_all, part), F32),
        shape((rows_all, part), F32),
        shape((4, blocks, half), F32),
    ]
    own_rows, normed_rows, pre, proj, attended, grad_gated, stats = call(
        forward_kernel, fwd_outs, fwd_args, 4 * rows_all * rows_all * part, limit=room
    )(
        scratch_shapes=[
            pltpu.VMEM((rows_all, 1), jnp.int32),
            pltpu.VMEM((rows_all, width), BF),
            pltpu.VMEM((heads, rows_all, part), BF),
            pltpu.VMEM((heads, rows_all, part), BF),
            pltpu.VMEM((part, rows_all), BF),
        ]
    )(*fwd_args)

    stats_of = direct([stats] * ctx, "ctx")

    def between_kernel(normed_ref, pre_ref, proj_ref, norm_t_ref, slope_ref, query_ref, key_ref, query_t_ref):
        masks = lane_masks()
        for tile in range(tiles):
            span = pl.ds(tile * TILE, TILE)
            norm_t_ref[:, tile * TILE : (tile + 1) * TILE] = jnp.transpose(normed_ref[span, :])
            slope_ref[span, :] = silu_grad(pre_ref[span, :])
            query = proj_ref[span, 2 * part : 3 * part] * jnp.asarray(0.5 * scale, BF)
            key = proj_ref[span, 3 * part :]
            for head in range(heads):
                query_ref[head, span, :] = jnp.where(masks[head], query, jnp.zeros_like(query))
                query_t_ref[head, :, tile * TILE : (tile + 1) * TILE] = jnp.transpose(query_ref[head, span, :])
                key_ref[head, span, :] = jnp.where(masks[head], key, jnp.zeros_like(key))

    between_args = (normed_rows, pre, proj)
    between_outs = [
        shape((width, rows_all), BF),
        shape((rows_all, 4 * part), F32),
        shape((heads, rows_all, part), BF),
        shape((heads, rows_all, part), BF),
        shape((heads, part, rows_all), BF),
    ]
    norm_t, slope, *head_parts = call(
        between_kernel, between_outs, between_args, 10 * rows_all * width, limit=room
    )()(*between_args)

    grad_count = 4 if packed else 2

    def proj_places(chunk):
        return [(at * proj_step, 2 * chunk + at) for at in range(2)]

    def out_places(chunk):
        return [(2 * proj_step + at * out_step, ctx // 2 * chunk + at) for at in range(ctx // 2)]

    def backward_kernel(*refs):
        stat_refs, cot_refs = refs[:ctx], refs[ctx : 2 * ctx]
        begin_ref, att_ref, gg_ref, slope_ref, proj_ref, norm_t_ref = refs[2 * ctx : 2 * ctx + 6]
        query_ref, key_ref, query_t_ref = refs[2 * ctx + 6 : 2 * ctx + 9]
        grad_refs, refs = refs[2 * ctx + 9 : 2 * ctx + 9 + grad_count], refs[2 * ctx + 9 + grad_count :]
        row_refs = refs[:ctx]
        grad_ref, dq_ref, gp_ref, gated_ref, late_ref, out_ref = refs[ctx:]
        mine = lax.axis_index("ctx")
        masks = lane_masks()

        def masked(values, head):
            return jnp.where(masks[head], values, jnp.zeros_like(values))

        means = [each[0] for each in stat_refs]
        mean = sum(means) / ctx
        spread_sum = sum(each[1] + part * (own - mean) ** 2 for each, own in zip(stat_refs, means))
        inverse = lax.rsqrt(spread_sum / width + EPS)
        grad_mean = sum(each[2] for each in stat_refs) / width
        cross = sum(each[3] + each[2] * (own - mean) for each, own in zip(stat_refs, means))
        cross_mean = inverse * cross / width
        for block in range(blocks):
            span = pl.ds(block * half, half)
            table = jnp.concatenate(
                [each[block : block + 1, :] for each in (mean, inverse, grad_mean, cross_mean)] * 2
            )
            columns = jnp.transpose(table)
            mean_c, inverse_c, grad_c, cross_c = (columns[:, each : each + 1] for each in range(4))
            normed = (att_ref[span, :] - mean_c) * inverse_c
            grad = gg_ref[span, :]
            update = proj_ref[span, :part].astype(F32)
            gated_ref[span, :] = (normed * update).astype(BF)
            grad_att = ((grad * update - grad_c - normed * cross_c) * inverse_c).astype(BF)
            gp_ref[span, :part] = (grad * normed * slope_ref[span, :part]).astype(BF)
            for head in range(heads):
                grad_ref[head, span, :] = masked(grad_att, head)
            dq_ref[span, :] = jnp.zeros((half, part), F32)
        out_term = jnp.zeros((part, width), F32)
        for rel in range(ctx):
            for side in range(2):
                here = slice(side * half, (side + 1) * half)
                gated = gated_ref[block_rows(mine ^ rel, side), :]
                row_refs[rel][here, 4 * part :] = gated
            out_term = out_term + tn_dot(row_refs[rel][:, 4 * part :], cot_refs[rel][:own_count, :])
        out_ref[...] = out_term.astype(BF)
        for key_at in range(tiles):
            key_span = pl.ds(key_at * TILE, TILE)
            key_pos = lax.broadcasted_iota(jnp.int32, (TILE, 1), 0) + key_at * TILE
            key = proj_ref[key_span, 3 * part :]
            value = proj_ref[key_span, part : 2 * part] * jnp.asarray(0.5 * scale, BF)
            grad_key = jnp.zeros((TILE, part), F32)
            grad_value = jnp.zeros((TILE, part), F32)
            for at in range(key_at, tiles):
                span = pl.ds(at * TILE, TILE)
                query_pos = lax.broadcasted_iota(jnp.int32, (1, TILE), 1) + at * TILE
                begin = jnp.concatenate(
                    [
                        begin_ref[each : each + 1, :]
                        for each in range(at * TILE // half, (at + 1) * TILE // half)
                    ],
                    axis=1,
                )
                allowed = key_pos >= begin
                if at == key_at:
                    allowed = allowed & (key_pos <= query_pos)
                grad_query = jnp.zeros((TILE, part), F32)
                for head in range(heads):
                    score = nn_dot(key, query_t_ref[head, :, at * TILE : (at + 1) * TILE])
                    tanh = jnp.tanh(score)
                    cross = score * tanh
                    weight = jnp.where(allowed, score + cross, 0.0).astype(BF)
                    grad_value = grad_value + nn_dot(weight, grad_ref[head, span, :])
                    grad_weight = nt_dot(value, grad_ref[head, span, :])
                    slope = (1.0 + tanh) * (1.0 + score - cross)
                    grad_score = jnp.where(allowed, grad_weight * slope, 0.0).astype(BF)
                    grad_key = grad_key + nn_dot(grad_score, query_ref[head, span, :])
                    grad_query = grad_query + tn_dot(grad_score, key_ref[head, key_span, :])
                dq_ref[span, :] = dq_ref[span, :] + grad_query
            gp_ref[key_span, part : 2 * part] = (
                grad_value * slope_ref[key_span, part : 2 * part]
            ).astype(BF)
            gp_ref[key_span, 3 * part :] = (
                grad_key * (2.0 / scale) * slope_ref[key_span, 3 * part :]
            ).astype(BF)
        for tile in range(tiles):
            span = pl.ds(tile * TILE, TILE)
            gp_ref[span, 2 * part : 3 * part] = (
                dq_ref[span, :] * slope_ref[span, 2 * part : 3 * part]
            ).astype(BF)
        for rel in range(ctx):
            for side in range(2):
                row_refs[rel][side * half : (side + 1) * half, : 4 * part] = gp_ref[
                    block_rows(mine ^ rel, side), :
                ]
        late_ref[...] = nn_dot(norm_t_ref[...], gp_ref[...]).astype(BF)
        if not packed:
            grad_refs[0][...] = late_ref[...]
            grad_refs[1][...] = out_ref[...]
            return
        mine = lax.axis_index("dp")
        for slot in range(dps):
            index = reverse_bits(slot, dps) ^ mine
            rows = pl.ds(pl.multiple_of(index * proj_step, proj_step), proj_step)
            out_rows = pl.ds(pl.multiple_of(index * out_step, out_step), out_step)
            for chunk in range(2):
                to = grad_refs[2 * chunk + slot // (dps // 2)].at[slot % (dps // 2)]
                for first, each in proj_places(chunk):
                    to[first : first + proj_step, :] = late_ref[rows, each * part : (each + 1) * part]
                for first, each in out_places(chunk):
                    to[first : first + out_step, :] = out_ref[out_rows, each * part : (each + 1) * part]

    bwd_args = (*stats_of, *cot_of, begin_of, attended, grad_gated, slope, proj, norm_t, *head_parts)
    if packed:
        bwd_outs = [shape((dps // 2, piece_rows, part), BF)] * 4
    else:
        bwd_outs = [shape((width, 4 * part), BF), shape((part, width), BF)]
    bwd_outs = bwd_outs + [shape((own_count, 5 * part), BF)] * ctx
    results = call(
        backward_kernel, bwd_outs, bwd_args, 10 * rows_all * rows_all * part, limit=room
    )(
        scratch_shapes=[
            pltpu.VMEM((heads, rows_all, part), BF),
            pltpu.VMEM((rows_all, part), F32),
            pltpu.VMEM((rows_all, 4 * part), BF),
            pltpu.VMEM((rows_all, part), BF),
            pltpu.VMEM((width, 4 * part), BF),
            pltpu.VMEM((part, width), BF),
        ]
    )(*bwd_args)

    grad_parts, row_parts = results[:grad_count], results[grad_count:]

    if not packed:
        rev = jnp.array([reverse_bits(each, dps) for each in range(dps)], jnp.int32)
        proj_blocks = grad_parts[0].reshape(dps, proj_step, 4, part).transpose(0, 2, 1, 3)
        out_blocks = grad_parts[1].reshape(dps, out_step, ctx, part).transpose(0, 2, 1, 3)
        grad_parts = []
        for chunk in range(2):
            pieces = jnp.concatenate(
                [
                    proj_blocks[:, 2 * chunk : 2 * chunk + 2].reshape(dps, -1, part),
                    out_blocks[:, ctx // 2 * chunk : ctx // 2 * (chunk + 1)].reshape(dps, -1, part),
                ],
                axis=1,
            )
            grad_parts += jnp.split(jnp.take(pieces, rev ^ me_dp, axis=0), 2)

    def add_kernel(keep_ref, got_ref, *out_refs):
        count = out_refs[0].shape[0]
        for at, ref in enumerate(out_refs):
            here = slice(at * count, (at + 1) * count)
            ref[...] = (keep_ref[here].astype(F32) + got_ref[here].astype(F32)).astype(BF)

    def exchange_kernel(keep_ref, got_ref, out_ref):
        for at in range(2):
            total = keep_ref[at].astype(F32) + got_ref[1 - at].astype(F32)
            out_ref[at] = total.astype(BF)

    def reduce_dp(keep, send):
        for bit in dp_bits[:-1]:
            got = swap(send, "dp", bit)
            count = keep.shape[0] // 2
            last = count == 1
            outs = [shape((2 if last else count, piece_rows, part), BF)] * (1 if last else 2)
            keep, *send = call(add_kernel, outs, (keep, got), keep.size)()(keep, got)
            send = send[0] if send else None
        got = swap(keep, "dp", dp_bits[-1])
        return call(exchange_kernel, [shape(keep.shape, BF)], (keep, got), keep.size)()(keep, got)[0]

    held = [reduce_dp(*grad_parts[2 * chunk : 2 * chunk + 2]) for chunk in range(2)]
    keys = [0, dp_bits[-1]]
    row_own = direct(row_parts, "ctx")

    def rows_kernel(*refs):
        part_refs, (rows_ref, cot_ref, weight_ref, out_weight_ref, layer_ref, grad_ref) = refs[:ctx], refs[ctx:]
        mine = lax.axis_index("ctx")
        rows = rows_ref[...].astype(F32)
        layer = rows
        grad = jnp.zeros((own_count, width), F32)
        for rel in range(ctx):
            column = mine ^ rel
            at = pl.ds(pl.multiple_of(column * part, part), part)
            layer = layer + nn_dot(part_refs[rel][:, 4 * part :], out_weight_ref[at, :])
            for each in range(4):
                grad = grad + nt_dot(
                    part_refs[rel][:, each * part : (each + 1) * part], weight_of(weight_ref, column, each)
                )
        layer_ref[...] = layer.astype(BF)
        normed, inverse = normalize(rows)
        mean_grad = jnp.mean(grad, axis=-1, keepdims=True)
        mean_cross = jnp.mean(grad * normed, axis=-1, keepdims=True)
        back = (grad - mean_grad - normed * mean_cross) * inverse
        grad_ref[...] = (cot_ref[...].astype(F32) + back).astype(BF)

    rows_args = tuple(row_own) + (own_rows, cotangent, weights, out_weight)
    layer_out, row_grads = call(
        rows_kernel, [shape((own_count, width), BF)] * 2, rows_args, 10 * own_count * width * width
    )()(*rows_args)

    for bit in dp_bits[-2:0:-1]:
        held = [jnp.concatenate([each, swap(each, "dp", bit)]) for each in held]
        keys = keys + [key | bit for key in keys]
    order = (ctx_bits, ctx_bits[::-1])
    arrays, holds = [], []
    groups = [[], [], []]
    for chunk in range(2):
        for rel, values in spread(held[chunk], "ctx", order[chunk]).items():
            arrays.append(values)
            holds.append([(chunk, rel, key) for key in keys])
            groups[0 if rel == 0 else 2 if rel == ctx - 1 else 1].append(len(holds) - 1)
    for group in groups:
        both = jnp.concatenate([arrays[each] for each in group])
        arrays.append(swap(both, "dp", 1))
        holds.append([(chunk, rel, key | 1) for each in group for chunk, rel, key in holds[each]])

    if packed:

        def finish_kernel(*refs):
            proj_ref, out_ref = refs[len(arrays) :]
            mine_ctx, mine_dp = lax.axis_index("ctx"), lax.axis_index("dp")
            for ref, pieces in zip(refs, holds):
                for at, (chunk, rel_ctx, rel_dp) in enumerate(pieces):
                    column, index = mine_ctx ^ rel_ctx, mine_dp ^ rel_dp
                    rows = pl.ds(pl.multiple_of(index * proj_step, proj_step), proj_step)
                    for first, each in proj_places(chunk):
                        lanes = pl.ds(pl.multiple_of(each * width + column * part, part), part)
                        proj_ref[rows, lanes] = ref[at, first : first + proj_step, :].astype(F32) * grad_scale
                    rows = pl.ds(pl.multiple_of(column * part + index * out_step, out_step), out_step)
                    for first, each in out_places(chunk):
                        out_ref[rows, each * part : (each + 1) * part] = (
                            ref[at, first : first + out_step, :].astype(F32) * grad_scale
                        )

        proj_grad, out_grad = call(
            finish_kernel,
            [shape((width, 4 * width), F32), shape((width, width), F32)],
            arrays,
            width * width * 10,
        )()(*arrays)
        return (layer_out, row_grads, proj_grad, out_grad)

    pieces = {key: array[at] for array, hold in zip(arrays, holds) for at, key in enumerate(hold)}
    table = jnp.stack(
        [
            jnp.stack([jnp.stack([pieces[chunk, c, d] for chunk in range(2)]) for d in range(dps)])
            for c in range(ctx)
        ]
    )
    table = jnp.take(table, jnp.arange(ctx) ^ me_ctx, axis=0)
    table = jnp.take(table, jnp.arange(dps) ^ me_dp, axis=1).astype(F32) * grad_scale
    proj_grad = (
        table[:, :, :, : 2 * proj_step]
        .reshape(ctx, dps, 4, proj_step, part)
        .transpose(1, 3, 2, 0, 4)
        .reshape(width, 4 * width)
    )
    out_grad = (
        table[:, :, :, 2 * proj_step :]
        .reshape(ctx, dps, ctx, out_step, part)
        .transpose(0, 1, 3, 2, 4)
        .reshape(width, width)
    )
    return (layer_out, row_grads, proj_grad, out_grad)


def solution(mesh):
    placed = (
        P(("dp", "ctx"), None),
        P(("dp", "ctx")),
        P(("dp", "ctx")),
        P("dp", None),
        P(),
        P(),
        P(("dp", "ctx"), None),
    )

    return jax.shard_map(
        local,
        mesh=mesh,
        in_specs=placed,
        out_specs=(P(("dp", "ctx"), None), P(("dp", "ctx"), None), P(), P()),
        check_vma=False,
    )
```
